32 devices in a mesh: pair: 8 (over z, core), aux: 4 (over y, x).
Axes of the slice: x: 2, y: 2, z: 4, core: 2. Of those that a mesh axis runs over, the one named last changes fastest.
Arguments:
- factors: bfloat16 [384, 16, 64, 128], P('aux', 'pair'), may hold values from -1.75 to 1.75
- pairs: int32 [80, 2], replicated, may hold values from 0 to 15, as said below
- shared: int32 [80, 4], P(None, 'aux'), may hold values 0 or 1
- owners: int32 [80], replicated, may hold values from 0 to 7, as said below
Outputs:
- exchange_matrix: float32 [16, 128, 2048], P('pair', 'aux')
- pair_tiles: float32 [8, 40, 128, 128], P('pair', None, 'aux')
The draws below stay inside these ranges and needn't reach their ends.
Inputs may be any that keep to these rules, and one draw needn't show every extreme that they name: Distinct pairs (a, b) with a <= b. `owners`: each device owns at most 40 pairs and one device owns exactly 40.
All inputs are finite; a program needn't handle non-finite values. No bound on the sum of `shared` on one device may be relied on, other than what follows from the above.
Results may differ from the reference program's by a relative error of at most 0.0003.
Values may be sent and summed in bfloat16 or wider, within the bound.
No kernel may reach another device: no remote copies, remote signals or barrier semaphores. Data moves between devices by JAX's collectives and lax.ppermute only.
A program may use at most 128 MiB of HBM per device.

```python
import jax
import jax.numpy as jnp
import numpy as np
from jax import lax

NTILE = 16
TILE = 128
OCC = 64
AUX_DEV = 96
NPAIRS = 80
NOWNERS = 8
NBLOCK = 4
PMAX = 40
NAUX = 384
NB = 2048


def draw_pairs(key, part):
    upper_rows, upper_cols = np.triu_indices(NTILE)
    table = jnp.asarray(np.stack([upper_rows, upper_cols], axis=1).astype(np.int32))
    order = jax.random.permutation(key, table.shape[0])[:NPAIRS]
    return table[order].astype(jnp.int32)


def draw_owners(key, part):
    busiest = jax.random.randint(jax.random.fold_in(key, 11), (), 0, NOWNERS)
    shuffle = jax.random.permutation(jax.random.fold_in(key, 23), NPAIRS)
    position = jnp.arange(NPAIRS, dtype=jnp.int32)
    spread = (busiest + 1 + (position - PMAX) % (NOWNERS - 1)) % NOWNERS
    by_position = jnp.where(position < PMAX, busiest, spread)
    return by_position[shuffle].astype(jnp.int32)


def with_ends(values, rng, low, largest):
    extent = values.shape
    spot = [jax.random.randint(jax.random.fold_in(rng, axis), (), 0, extent[axis]) for axis in range(len(extent))]
    values = values.at[tuple(spot)].set(low)
    longest = extent.index(max(extent))
    spot[longest] = (spot[longest] + 1) % extent[longest]
    return values.at[tuple(spot)].set(largest)


def strengthened(entries, rng, source, target, blocks, factor):
    def block_of(dim):
        return (jnp.arange(entries.shape[dim]) // (entries.shape[dim] // blocks)).reshape((-1,) + (1,) * (entries.ndim - 1 - dim))

    one_side = jax.random.permutation(rng, blocks)[block_of(target)]
    far = (block_of(target) + blocks // 2) % blocks
    return jnp.where((block_of(source) == one_side) | (block_of(source) == far), factor * entries, entries)


def block_scale(rng, shape, cuts, smallest, top_value):
    loudness, own = 1.0, jax.random.fold_in(rng, 6)
    for dim, shards_of in cuts:
        steps = jnp.exp(jax.random.uniform(jax.random.fold_in(own, dim), (shards_of,), jnp.float32, smallest / len(cuts), top_value / len(cuts)))
        loudness = loudness * jnp.repeat(steps, shape[dim] // shards_of).reshape([-1 if axis == dim else 1 for axis in range(len(shape))])
    return loudness


def gaussian_with(stream_key, extent, width, reach, shards, heavy, held_as=jnp.bfloat16):
    drawn = width * jax.random.normal(stream_key, extent, jnp.float32)
    if shards:
        drawn = drawn * block_scale(stream_key, extent, shards, -0.22, 0.18)
    return jnp.clip(strengthened(drawn, jax.random.fold_in(stream_key, 3), *heavy), -reach, reach).astype(held_as)


def setup_inputs(seed: int = 0) -> dict:
    key_of = jax.random.split(jax.random.key(seed), 5)
    return {
        "factors": gaussian_with(key_of[0], (NAUX, NTILE, OCC, TILE), ((NAUX * OCC) ** -0.25), 1.75, ((0, 4), (1, 8)), (0, 3, 4, 2.0)),
        "pairs": draw_pairs(jax.random.fold_in(key_of[4], 71), 0),
        "shared": with_ends((jax.random.randint(key_of[2], (NPAIRS, NBLOCK), 0, 4) < 3).astype(jnp.int32), jax.random.fold_in(key_of[2], 1), 0, 1),
        "owners": draw_owners(jax.random.fold_in(key_of[4], 71), 0),
    }


def reference(factors, pairs, shared, owners):
    def one_pair(index):
        left_id = pairs[index, 0]
        right_id = pairs[index, 1]
        left_block = lax.dynamic_index_in_dim(factors, left_id, 1, keepdims=False).astype(jnp.float32)
        right_block = lax.dynamic_index_in_dim(factors, right_id, 1, keepdims=False).astype(jnp.float32)
        weight = jnp.repeat(shared[index].astype(jnp.float32), AUX_DEV)
        left_block = left_block * weight[:, None, None]
        return jnp.einsum("pim,pin->mn", left_block, right_block, precision=lax.Precision.HIGHEST)

    kpairs = lax.map(one_pair, jnp.arange(NPAIRS, dtype=jnp.int32))

    def place(index, matrix):
        left_id = pairs[index, 0]
        right_id = pairs[index, 1]
        block = kpairs[index]
        matrix = lax.dynamic_update_slice(matrix, block.T, (right_id * TILE, left_id * TILE))
        matrix = lax.dynamic_update_slice(matrix, block, (left_id * TILE, right_id * TILE))
        return matrix

    matrix = lax.fori_loop(0, NPAIRS, place, jnp.zeros((NB, NB), jnp.float32))
    pair_ids = jnp.arange(NPAIRS, dtype=jnp.int32)
    same_owner = owners[:, None] == owners[None, :]
    owner_rank = jnp.sum((same_owner & (pair_ids[None, :] < pair_ids[:, None])).astype(jnp.int32), axis=1).astype(jnp.int32)
    tiles_out = jnp.zeros((NOWNERS, PMAX, TILE, TILE), jnp.float32).at[owners, owner_rank].set(kpairs)
    return matrix.reshape(NTILE, TILE, NB), tiles_out
```

```python
import jax
import jax.numpy as jnp
from jax import lax
from jax.experimental import pallas as pl
from jax.experimental.pallas import tpu as pltpu
from jax.sharding import PartitionSpec as P

VMEM_LIMIT = 48 << 20


def swap(value, axis, size, step):
    return lax.ppermute(value, axis, [(i, i ^ step) for i in range(size)])


def contract_kernel(left, right, weight, *refs):
    *parts, out, plain, turned = refs
    count = out.shape[0]
    depth, here, orbitals, width = parts[0].shape
    for step, part in enumerate(parts):
        for tile in range(here):
            block = part[:, tile].reshape(depth * orbitals, width)
            plain[step * here + tile] = block
            turned[step * here + tile] = block.T

    def one(index, carry):
        @pl.when(weight[index] != 0)
        def _():
            out[index] = jnp.dot(
                turned[left[index]], plain[right[index]], preferred_element_type=jnp.float32
            )

        @pl.when(weight[index] == 0)
        def _():
            out[index] = jnp.zeros((width, width), jnp.float32)

        return carry

    lax.fori_loop(0, count, one, 0)


def contract(parts, left, right, weight):
    depth, here, orbitals, width = parts[0].shape
    tiles = len(parts) * here
    count = left.shape[0]
    return pl.pallas_call(
        contract_kernel,
        out_shape=jax.ShapeDtypeStruct((count, width, width), jnp.float32),
        grid_spec=pltpu.PrefetchScalarGridSpec(
            num_scalar_prefetch=3,
            grid=(),
            in_specs=[pl.BlockSpec(memory_space=pltpu.VMEM)] * len(parts),
            out_specs=pl.BlockSpec(memory_space=pltpu.VMEM),
            scratch_shapes=[
                pltpu.VMEM((tiles, depth * orbitals, width), jnp.bfloat16),
                pltpu.VMEM((tiles, width, depth * orbitals), jnp.bfloat16),
            ],
        ),
        compiler_params=pltpu.CompilerParams(vmem_limit_bytes=VMEM_LIMIT),
    )(left, right, weight, *parts)


def turn_kernel(source, out):
    for group in range(source.shape[0]):
        out[group] = source[group].T


def turn(source):
    return pl.pallas_call(
        turn_kernel,
        out_shape=jax.ShapeDtypeStruct(source.shape, source.dtype),
        in_specs=[pl.BlockSpec(memory_space=pltpu.VMEM)],
        out_specs=pl.BlockSpec(memory_space=pltpu.VMEM),
        compiler_params=pltpu.CompilerParams(vmem_limit_bytes=VMEM_LIMIT),
    )(source)


def place_kernel(columns, kinds, sources, slots, direct, mirror, matrix, tiles):
    here, rows, _ = matrix.shape
    width = direct.shape[-1]
    columns_here = mirror.shape[0]
    pack = width // rows
    tile_count = matrix.shape[2] // width
    lane = lax.broadcasted_iota(jnp.int32, (rows, width), 1) // rows
    for tile in range(here):

        def one(other, carry):
            spot = tile * tile_count + other
            kind = kinds[spot]
            source = sources[spot]
            target = pl.ds(pl.multiple_of(other * width, width), width)

            @pl.when(kind == 0)
            def _():
                matrix[tile, :, target] = jnp.zeros((rows, width), jnp.float32)

            @pl.when(kind == 1)
            def _():
                matrix[tile, :, target] = direct[source]

            @pl.when(kind == 2)
            def _():
                group = source // pack
                place = source - group * pack
                total = jnp.zeros((rows, width), jnp.float32)
                for step in range(columns_here):
                    column = columns[step]
                    shift = ((column - place + pack) % pack) * rows
                    moved = pltpu.roll(mirror[step, group], shift, 1)
                    total = jnp.where(lane == column, moved, total)
                matrix[tile, :, target] = total

            return carry

        lax.fori_loop(0, tile_count, one, 0)

    def fill(slot, carry):
        source = slots[slot]

        @pl.when(source < 0)
        def _():
            tiles[0, slot] = jnp.zeros((rows, width), jnp.float32)

        @pl.when(source >= 0)
        def _():
            tiles[0, slot] = direct[source]

        return carry

    lax.fori_loop(0, tiles.shape[1], fill, 0)


def place(columns, kinds, sources, slots, direct, mirror, here, tile_count):
    _, rows, width = direct.shape
    return pl.pallas_call(
        place_kernel,
        out_shape=(
            jax.ShapeDtypeStruct((here, rows, tile_count * width), jnp.float32),
            jax.ShapeDtypeStruct((1, slots.shape[0], rows, width), jnp.float32),
        ),
        grid_spec=pltpu.PrefetchScalarGridSpec(
            num_scalar_prefetch=4,
            grid=(),
            in_specs=[pl.BlockSpec(memory_space=pltpu.VMEM)] * 2,
            out_specs=[pl.BlockSpec(memory_space=pltpu.VMEM)] * 2,
        ),
        compiler_params=pltpu.CompilerParams(vmem_limit_bytes=VMEM_LIMIT),
    )(columns, kinds, sources, slots, direct, mirror)


def take(value, index):
    return lax.dynamic_index_in_dim(value, index, 0, keepdims=False)


def body(factors, pairs, shared, owners):
    aux_rows, here, orbitals, width = factors.shape
    pair_size = lax.axis_size("pair")
    aux_size = lax.axis_size("aux")
    chips = pair_size // 2
    tile_count = here * pair_size
    pair_count = pairs.shape[0]
    rows = width // aux_size
    slot_count = 4 * (pair_count // pair_size)
    me = lax.axis_index("pair")
    core = me % 2
    chip = me // 2
    column = lax.axis_index("aux")
    depth = aux_rows // pair_size
    pack = aux_size
    unit = max(pack, chips)
    half = -(-(-(-pair_count // 2)) // unit) * unit
    share = half // chips
    padded = 2 * half

    pair_ids = jnp.arange(pair_count, dtype=jnp.int32)
    lefts, rights = pairs[:, 0], pairs[:, 1]
    same_owner = owners[:, None] == owners[None, :]
    rank = jnp.sum(
        (same_owner & (pair_ids[None, :] < pair_ids[:, None])).astype(jnp.int32), axis=1
    )
    left_slots = ((lefts // here) ^ me) * here + lefts % here
    right_slots = ((rights // here) ^ me) * here + rights % here
    weights = shared[:, 0]
    tables = jnp.pad(
        jnp.stack([left_slots, right_slots, weights]), ((0, 0), (0, padded - pair_count))
    ).reshape(3, 2, half)
    mine = lax.dynamic_index_in_dim(tables, core, 1, keepdims=False)
    theirs = lax.dynamic_index_in_dim(tables, 1 - core, 1, keepdims=False)

    local = pair_ids % half
    part_core = pair_ids // half
    final_pos = (part_core ^ core) * half + ((local // share) ^ chip) * share + local % share
    my_rows = me * here + jnp.arange(here, dtype=jnp.int32)
    others = jnp.arange(tile_count, dtype=jnp.int32)
    is_direct = (lefts == my_rows[:, None, None]) & (rights == others[None, :, None])
    is_mirror = (rights == my_rows[:, None, None]) & (lefts == others[None, :, None])
    any_direct = jnp.any(is_direct, axis=-1)
    any_mirror = jnp.any(is_mirror, axis=-1)
    kinds = jnp.where(any_direct, 1, jnp.where(any_mirror, 2, 0)).astype(jnp.int32).reshape(-1)
    chosen = jnp.where(any_direct[..., None], is_direct, is_mirror)
    sources = jnp.sum(jnp.where(chosen, final_pos, 0), axis=-1).astype(jnp.int32).reshape(-1)
    slot_ids = jnp.arange(slot_count, dtype=jnp.int32)
    matches = (owners[None, :] == me) & (rank[None, :] == slot_ids[:, None])
    slots = jnp.sum(jnp.where(matches, final_pos + 1, 0), axis=1).astype(jnp.int32) - 1
    columns = column ^ jnp.arange(aux_size, dtype=jnp.int32)

    pieces = factors.reshape(pair_size, depth, here, orbitals, width)
    parts = [take(pieces, me)]
    for step in range(1, pair_size):
        parts.append(swap(take(pieces, me ^ step), "pair", pair_size, step))

    given = contract(parts, *theirs)
    kept = contract(parts, *mine)
    chip_sum = kept + swap(given, "pair", pair_size, 1)

    by_column = chip_sum.reshape(half, aux_size, rows, width)

    def column_rows(step):
        return lax.dynamic_index_in_dim(by_column, column ^ step, 1, keepdims=False)

    summed = column_rows(0)
    arrived = [swap(column_rows(step), "aux", aux_size, step) for step in range(1, aux_size)]
    for value in arrived:
        summed = summed + value

    by_chip = summed.reshape(chips, share, rows, width)
    arrived = [
        swap(take(by_chip, chip ^ step), "pair", pair_size, 2 * step) for step in range(1, chips)
    ]
    total = take(by_chip, chip)
    for value in arrived:
        total = total + value

    line = [total] + [swap(total, "pair", pair_size, 2 * step) for step in range(1, chips)]
    own_direct = jnp.concatenate(line, axis=0)
    other_direct = swap(own_direct, "pair", pair_size, 1)

    turned = turn(own_direct.reshape(half // pack, pack * rows, width))
    turned = turned.reshape(half // pack, aux_size, rows, width)

    def turned_rows(step):
        return lax.dynamic_index_in_dim(turned, column ^ step, 1, keepdims=False)

    own_mirror = jnp.stack(
        [turned_rows(0)]
        + [swap(turned_rows(step), "aux", aux_size, step) for step in range(1, aux_size)]
    )
    other_mirror = swap(own_mirror, "pair", pair_size, 1)
    direct = jnp.concatenate([own_direct, other_direct], axis=0)
    mirror = jnp.concatenate([own_mirror, other_mirror], axis=1)
    return place(columns, kinds, sources, slots, direct, mirror, here, tile_count)


def solution(mesh):
    placed = (P("aux", "pair", None, None), P(), P(None, "aux"), P())
    return jax.shard_map(
        body,
        mesh=mesh,
        in_specs=placed,
        out_specs=(P("pair", "aux", None), P("pair", None, "aux", None)),
        check_vma=False,
    )
```

```python
import jax
import jax.numpy as jnp
from jax import lax
from jax.experimental import pallas as pl
from jax.experimental.pallas import tpu as pltpu
from jax.sharding import PartitionSpec as P

VMEM_LIMIT = 24 << 20


def swap(value, axis, size, step):
    return lax.ppermute(value, axis, [(i, i ^ step) for i in range(size)])


def contract_kernel(left, right, weight, column, tiles, out):
    count = out.shape[1]
    rows = out.shape[2]

    def one(index, carry):
        block = lax.dot_general(
            tiles[left[index]],
            tiles[right[index]],
            (((0,), (0,)), ((), ())),
            preferred_element_type=jnp.float32,
        ) * weight[index].astype(jnp.float32)
        for step in range(out.shape[0]):
            out[column[0] ^ step, index] = block[step * rows : (step + 1) * rows]
        return carry

    lax.fori_loop(0, count, one, 0, unroll=4)


def contract(tiles, table, column, aux_size):
    width = tiles.shape[-1]
    count = table.shape[1]
    return pl.pallas_call(
        contract_kernel,
        out_shape=jax.ShapeDtypeStruct((aux_size, count, width // aux_size, width), jnp.float32),
        grid_spec=pltpu.PrefetchScalarGridSpec(
            num_scalar_prefetch=4,
            grid=(),
            in_specs=[pl.BlockSpec(memory_space=pltpu.VMEM)],
            out_specs=pl.BlockSpec(memory_space=pltpu.VMEM),
        ),
        compiler_params=pltpu.CompilerParams(vmem_limit_bytes=VMEM_LIMIT),
    )(table[0], table[1], table[2], column.reshape(1), tiles)


def gather_kernel(targets, *refs):
    *groups, out = refs
    base = 0
    per_group = len(groups) // 3
    for part in range(3):
        first, *rest = groups[part * per_group : (part + 1) * per_group]

        def one(index, carry, first=first, rest=rest, base=base):
            total = first[0, index]
            for ref in rest:
                total = total + ref[index]
            out[targets[base + index]] = total
            return carry

        lax.fori_loop(0, first.shape[1], one, 0, unroll=4)
        base += first.shape[1]


def gather_sums(targets, groups):
    flat = [value for group in groups for value in group]
    _, _, rows, width = flat[0].shape
    return pl.pallas_call(
        gather_kernel,
        out_shape=jax.ShapeDtypeStruct((targets.shape[0], rows, width), jnp.float32),
        grid_spec=pltpu.PrefetchScalarGridSpec(
            num_scalar_prefetch=1,
            grid=(),
            in_specs=[pl.BlockSpec(memory_space=pltpu.VMEM)] * len(flat),
            out_specs=pl.BlockSpec(memory_space=pltpu.VMEM),
        ),
        compiler_params=pltpu.CompilerParams(vmem_limit_bytes=VMEM_LIMIT),
    )(targets, *flat)


def turn_kernel(source, out):
    for group in range(source.shape[0]):
        out[group] = source[group].T


def turn(source):
    return pl.pallas_call(
        turn_kernel,
        out_shape=jax.ShapeDtypeStruct(source.shape, source.dtype),
        in_specs=[pl.BlockSpec(memory_space=pltpu.VMEM)],
        out_specs=pl.BlockSpec(memory_space=pltpu.VMEM),
        compiler_params=pltpu.CompilerParams(vmem_limit_bytes=VMEM_LIMIT),
    )(source)


def place_kernel(columns, kinds, sources, slots, direct, mirror, matrix, tiles):
    here, rows, _ = matrix.shape
    width = direct.shape[-1]
    columns_here = mirror.shape[0]
    pack = width // rows
    tile_count = matrix.shape[2] // width
    lane = lax.broadcasted_iota(jnp.int32, (rows, width), 1) // rows
    for tile in range(here):

        def one(other, carry):
            spot = tile * tile_count + other
            kind = kinds[spot]
            source = sources[spot]
            target = pl.ds(pl.multiple_of(other * width, width), width)

            @pl.when(kind == 0)
            def _():
                matrix[tile, :, target] = jnp.zeros((rows, width), jnp.float32)

            @pl.when(kind == 1)
            def _():
                matrix[tile, :, target] = direct[source]

            @pl.when(kind == 2)
            def _():
                group = source // pack
                place = source - group * pack
                total = jnp.zeros((rows, width), jnp.float32)
                for step in range(columns_here):
                    column = columns[step]
                    shift = ((column - place + pack) % pack) * rows
                    moved = pltpu.roll(mirror[step, group], shift, 1)
                    total = jnp.where(lane == column, moved, total)
                matrix[tile, :, target] = total

            return carry

        lax.fori_loop(0, tile_count, one, 0)

    def fill(slot, carry):
        source = slots[slot]

        @pl.when(source < 0)
        def _():
            tiles[0, slot] = jnp.zeros((rows, width), jnp.float32)

        @pl.when(source >= 0)
        def _():
            tiles[0, slot] = direct[source]

        return carry

    lax.fori_loop(0, tiles.shape[1], fill, 0)


def place(columns, kinds, sources, slots, direct, mirror, here, tile_count):
    _, rows, width = direct.shape
    return pl.pallas_call(
        place_kernel,
        out_shape=(
            jax.ShapeDtypeStruct((here, rows, tile_count * width), jnp.float32),
            jax.ShapeDtypeStruct((1, slots.shape[0], rows, width), jnp.float32),
        ),
        grid_spec=pltpu.PrefetchScalarGridSpec(
            num_scalar_prefetch=4,
            grid=(),
            in_specs=[pl.BlockSpec(memory_space=pltpu.VMEM)] * 2,
            out_specs=[pl.BlockSpec(memory_space=pltpu.VMEM)] * 2,
        ),
        compiler_params=pltpu.CompilerParams(vmem_limit_bytes=VMEM_LIMIT),
    )(columns, kinds, sources, slots, direct, mirror)


def take(value, index):
    return lax.dynamic_index_in_dim(value, index, 0, keepdims=False)


def arrival_order(chips, here):
    far = [step for step in range(1, chips)]
    if chips == 4:
        far = [2, 1, 3]
    order = [(step, inner) for step in far[:2] for inner in range(here)]
    if len(far) > 1:
        order = [(step, inner) for inner in range(here) for step in far[:2]]
    return order + [(step, inner) for step in far[2:] for inner in range(here)]


def body(factors, pairs, shared, owners):
    aux_rows, here, orbitals, width = factors.shape
    pair_size = lax.axis_size("pair")
    aux_size = lax.axis_size("aux")
    chips = pair_size // 2
    tile_count = here * pair_size
    pair_count = pairs.shape[0]
    rows = width // aux_size
    slot_count = 4 * (pair_count // pair_size)
    me = lax.axis_index("pair")
    core = me % 2
    chip = me // 2
    column = lax.axis_index("aux")
    depth = aux_rows // chips
    pack = aux_size
    unit = max(pack, chips)
    half = -(-(-(-pair_count // 2)) // unit) * unit
    share = half // chips
    padded = 2 * half

    pair_ids = jnp.arange(pair_count, dtype=jnp.int32)
    lefts, rights = pairs[:, 0], pairs[:, 1]
    same_owner = owners[:, None] == owners[None, :]
    rank = jnp.sum(
        (same_owner & (pair_ids[None, :] < pair_ids[:, None])).astype(jnp.int32), axis=1
    )
    order = arrival_order(chips, here)
    tile_ids = jnp.arange(tile_count, dtype=jnp.int32)
    tile_chip = tile_ids // (2 * here) ^ chip
    tile_core = (tile_ids // here) % 2
    tile_spot = tile_ids % here
    arrival = jnp.where(tile_chip == 0, tile_spot * 2 + (tile_core ^ core), 0)
    rank_of = jnp.zeros_like(arrival)
    for spot, (step, inner) in enumerate(order):
        hit = (tile_chip == step) & (tile_spot == inner)
        last = spot == len(order) - 1
        lane = tile_core if last else tile_core ^ core
        arrival = jnp.where(hit, 2 * here + 2 * spot + lane, arrival)
        rank_of = jnp.where(hit, 1 + spot + (tile_core if last else 0), rank_of)
    left_slots = jnp.sum(jnp.where(lefts[:, None] == tile_ids, arrival, 0), axis=1)
    right_slots = jnp.sum(jnp.where(rights[:, None] == tile_ids, arrival, 0), axis=1)
    left_rank = jnp.sum(jnp.where(lefts[:, None] == tile_ids, rank_of, 0), axis=1)
    right_rank = jnp.sum(jnp.where(rights[:, None] == tile_ids, rank_of, 0), axis=1)
    ready = jnp.maximum(left_rank, right_rank)
    values = jnp.stack([left_slots, right_slots, shared[:, 0], ready])
    values = jnp.pad(values, ((0, 0), (0, padded - pair_count)))
    values = values.at[3, pair_count:].set(64) if padded > pair_count else values
    values = lax.dynamic_index_in_dim(values.reshape(4, 2, half), core, 1, keepdims=False)
    local_ids = jnp.arange(half, dtype=jnp.int32)
    key = values[3] * half + local_ids
    spot_of = jnp.sum((key[None, :] < key[:, None]).astype(jnp.int32), axis=1)
    sorter = spot_of[None, :] == local_ids[:, None]
    target_of = ((local_ids // share) ^ chip) * share + local_ids % share
    fields = jnp.concatenate([values[:3], target_of[None]])
    fields = jnp.sum(jnp.where(sorter[None], fields[:, None, :], 0), axis=2).astype(jnp.int32)
    real_half = -(-pair_count // 2)
    all_pairs = tile_count * (tile_count + 1) // 2
    bounds = [0]
    for missing in (2, 1):
        known = tile_count - missing
        bounds.append(max(1, real_half - (all_pairs - known * (known + 1) // 2)))
    bounds.append(half)

    local = pair_ids % half
    part_core = pair_ids // half
    final_pos = (part_core ^ core) * half + ((local // share) ^ chip) * share + local % share
    my_rows = me * here + jnp.arange(here, dtype=jnp.int32)
    others = jnp.arange(tile_count, dtype=jnp.int32)
    is_direct = (lefts == my_rows[:, None, None]) & (rights == others[None, :, None])
    is_mirror = (rights == my_rows[:, None, None]) & (lefts == others[None, :, None])
    any_direct = jnp.any(is_direct, axis=-1)
    any_mirror = jnp.any(is_mirror, axis=-1)
    kinds = jnp.where(any_direct, 1, jnp.where(any_mirror, 2, 0)).astype(jnp.int32).reshape(-1)
    chosen = jnp.where(any_direct[..., None], is_direct, is_mirror)
    sources = jnp.sum(jnp.where(chosen, final_pos, 0), axis=-1).astype(jnp.int32).reshape(-1)
    slot_ids = jnp.arange(slot_count, dtype=jnp.int32)
    matches = (owners[None, :] == me) & (rank[None, :] == slot_ids[:, None])
    slots = jnp.sum(jnp.where(matches, final_pos + 1, 0), axis=1).astype(jnp.int32) - 1
    columns = column ^ jnp.arange(aux_size, dtype=jnp.int32)

    pieces = factors.reshape(chips, depth, here, orbitals, width)

    def outgoing(step, inner):
        return take(pieces[:, :, inner], chip ^ step).reshape(depth * orbitals, width)

    tiles = []
    for inner in range(here):
        block = outgoing(0, inner)
        tiles += [block, swap(block, "pair", pair_size, 1)]
    for step, inner in order[:-1]:
        block = swap(outgoing(step, inner), "pair", pair_size, 2 * step)
        tiles += [block, swap(block, "pair", pair_size, 1)]
    step, inner = order[-1]
    last_block = outgoing(step, inner)
    late = []
    for lane in range(2):
        there = [(2 * i + lane, 2 * (i ^ step) + lane) for i in range(chips)]
        block = lax.ppermute(last_block, "pair", there)
        across = lax.ppermute(block, "pair", [(2 * i + lane, 2 * i + 1 - lane) for i in range(chips)])
        late.append(jnp.where(core == lane, block, across))

    store = jnp.stack(tiles + [jnp.zeros_like(tiles[0])] * 2)
    groups = []
    for part in range(3):
        if part:
            store = lax.dynamic_update_index_in_dim(
                store, late[part - 1], tile_count - 3 + part, 0
            )
        blocks = contract(store, fields[:3, bounds[part] : bounds[part + 1]], column, aux_size)
        groups.append(
            [blocks] + [swap(blocks[step], "aux", aux_size, step) for step in range(1, aux_size)]
        )
    summed = gather_sums(fields[3], groups)

    by_chip = summed.reshape(chips, share, rows, width)
    arrived = [swap(by_chip[step], "pair", pair_size, 2 * step) for step in range(1, chips)]
    total = by_chip[0]
    for value in arrived:
        total = total + value

    line = [total] + [swap(total, "pair", pair_size, 2 * step) for step in range(1, chips)]
    own_direct = jnp.concatenate(line, axis=0)
    other_direct = swap(own_direct, "pair", pair_size, 1)

    turned = turn(own_direct.reshape(half // pack, pack * rows, width))
    turned = turned.reshape(half // pack, aux_size, rows, width)

    def turned_rows(step):
        return lax.dynamic_index_in_dim(turned, column ^ step, 1, keepdims=False)

    own_mirror = jnp.stack(
        [turned_rows(0)]
        + [swap(turned_rows(step), "aux", aux_size, step) for step in range(1, aux_size)]
    )
    other_mirror = swap(own_mirror, "pair", pair_size, 1)
    direct = jnp.concatenate([own_direct, other_direct], axis=0)
    mirror = jnp.concatenate([own_mirror, other_mirror], axis=1)
    return place(columns, kinds, sources, slots, direct, mirror, here, tile_count)


def solution(mesh):
    placed = (P("aux", "pair", None, None), P(), P(None, "aux"), P())
    return jax.shard_map(
        body,
        mesh=mesh,
        in_specs=placed,
        out_specs=(P("pair", "aux", None), P("pair", None, "aux", None)),
        check_vma=False,
    )
```

```python
import functools

import jax
import jax.numpy as jnp
from jax import lax
from jax.experimental import pallas as pl
from jax.experimental.pallas import tpu as pltpu
from jax.sharding import PartitionSpec as P

VMEM_LIMIT = 24 << 20
TINY = pl.CostEstimate(flops=1, transcendentals=0, bytes_accessed=1)


def swap(value, axis, size, step):
    return lax.ppermute(value, axis, [(i, i ^ step) for i in range(size)])


def contract_kernel(spots, left, right, weight, column, *refs):
    *parts, out, tiles = refs
    parts = parts[: len(spots)]
    count = out.shape[1]
    rows = out.shape[2]
    length, width = tiles.shape[1:]
    for spot, part in zip(spots, parts):
        for inner in range(part.shape[1]):
            tiles[spot + inner] = part[:, inner].reshape(length, width)

    def one(index, carry):
        block = lax.dot_general(
            tiles[left[index]],
            tiles[right[index]],
            (((0,), (0,)), ((), ())),
            preferred_element_type=jnp.float32,
        ) * weight[index].astype(jnp.float32)
        for step in range(out.shape[0]):
            out[column[0] ^ step, index] = block[step * rows : (step + 1) * rows]
        return carry

    lax.fori_loop(0, count, one, 0, unroll=4)


def contract(parts, table, column, tile_count, aux_size, earlier):
    spots, values = zip(*parts)
    depth, _, orbitals, width = values[0].shape
    count = table.shape[1]
    return pl.pallas_call(
        functools.partial(contract_kernel, spots),
        out_shape=jax.ShapeDtypeStruct((aux_size, count, width // aux_size, width), jnp.float32),
        grid_spec=pltpu.PrefetchScalarGridSpec(
            num_scalar_prefetch=4,
            grid=(),
            in_specs=[pl.BlockSpec(memory_space=pltpu.VMEM)] * len(values)
            + [pl.BlockSpec(memory_space=pl.ANY)] * len(earlier),
            out_specs=pl.BlockSpec(memory_space=pltpu.VMEM),
            scratch_shapes=[pltpu.VMEM((tile_count, depth * orbitals, width), values[0].dtype)],
        ),
        cost_estimate=TINY,
        compiler_params=pltpu.CompilerParams(vmem_limit_bytes=VMEM_LIMIT),
    )(table[0], table[1], table[2], column.reshape(1), *values, *earlier)


LEVELS = 32766.0


def extra_blocks(count, rows):
    return -(-count // rows)


def packed_shape(count, rows, width):
    return jax.ShapeDtypeStruct((count + extra_blocks(count, rows), rows, width), jnp.int16)


def pack_block(block, factor):
    return jnp.round(block * factor).astype(jnp.int32).astype(jnp.int16)


def unpack_block(block, scale):
    return block.astype(jnp.int32).astype(jnp.float32) * scale


def load_scales(packed, count, scales):
    rows = packed.shape[1]
    for extra in range(extra_blocks(count, rows)):
        steps = packed[count + extra].astype(jnp.int32).astype(jnp.float32)
        scales[pl.ds(extra * rows, rows), :] = jnp.exp2(steps * (1 / 256)) * (1 / LEVELS)


def store_scales(packed, count, tops):
    rows = packed.shape[1]
    for extra in range(extra_blocks(count, rows)):
        here = pl.ds(extra * rows, rows)
        steps = jnp.ceil(jnp.log2(jnp.maximum(tops[here, :], 1e-30)) * 256) + 2
        packed[count + extra] = steps.astype(jnp.int32).astype(jnp.int16)
        tops[here, :] = jnp.exp2(steps * (-1 / 256)) * LEVELS


def top_of(block):
    return jnp.max(jnp.abs(block), axis=0, keepdims=True)


def loop(count, step, unroll=4):
    lax.fori_loop(0, count, lambda index, carry: (step(index), carry)[1], 0, unroll=unroll)


def split_kernel(kept, across, own, *refs):
    *outs, tops, total = refs
    count = own.shape[0]

    def keep(index):
        own[index] = kept[0, index] + across[0, index]

    loop(count, keep)
    for step, out in enumerate(outs):

        def add(index, step=step):
            block = kept[step + 1, index] + across[step + 1, index]
            total[index] = block
            tops[pl.ds(index, 1), :] = top_of(block)

        loop(count, add)
        store_scales(out, count, tops)

        def put(index, out=out):
            out[index] = pack_block(total[index], tops[pl.ds(index, 1), :])

        loop(count, put)


def scale_scratch(count, rows, width):
    return pltpu.VMEM((extra_blocks(count, rows) * rows, width), jnp.float32)


VMEM_SPEC = pl.BlockSpec(memory_space=pltpu.VMEM)
PARAMS = pltpu.CompilerParams(vmem_limit_bytes=VMEM_LIMIT)


def split_columns(kept, across):
    columns, count, rows, width = kept.shape
    return pl.pallas_call(
        split_kernel,
        out_shape=[jax.ShapeDtypeStruct((count, rows, width), jnp.float32)]
        + [packed_shape(count, rows, width)] * (columns - 1),
        in_specs=[VMEM_SPEC] * 2,
        out_specs=[VMEM_SPEC] * columns,
        scratch_shapes=[
            scale_scratch(count, rows, width),
            pltpu.VMEM((count, rows, width), jnp.float32),
        ],
        cost_estimate=TINY,
        compiler_params=PARAMS,
    )(kept, across)


def combine_kernel(counts, arrivals, keep_own, targets, *refs):
    flat, refs = refs[: len(counts) * (arrivals + 1)], refs[len(counts) * (arrivals + 1) :]
    outs, (total, tops, *scales) = refs[: -2 - arrivals], refs[-2 - arrivals :]
    share = outs[-1].shape[0] - extra_blocks_of(outs[-1])
    base = 0
    for part, count in enumerate(counts):
        own, *others = flat[part * (arrivals + 1) : (part + 1) * (arrivals + 1)]
        for other, scale in zip(others, scales):
            load_scales(other, count, scale)

        def add(index, own=own, others=others, base=base):
            block = own[index]
            for other, scale in zip(others, scales):
                block = block + unpack_block(other[index], scale[pl.ds(index, 1), :])
            total[targets[base + index]] = block

        loop(count, add)
        base += count
    packs = outs
    if keep_own:
        packs = outs[1:]

        def keep(index):
            outs[0][index] = total[index]

        loop(share, keep)
    for spot, out in enumerate(packs):
        start = (spot + 1) * share if keep_own else spot * share

        def look(index, start=start):
            tops[pl.ds(index, 1), :] = top_of(total[start + index])

        loop(share, look)
        store_scales(out, share, tops)

        def put(index, out=out, start=start):
            out[index] = pack_block(total[start + index], tops[pl.ds(index, 1), :])

        loop(share, put)


def extra_blocks_of(packed):
    blocks, rows = packed.shape[:2]
    count = next(n for n in range(blocks + 1) if n + extra_blocks(n, rows) == blocks)
    return blocks - count


def combine(targets, groups, share, keep_own):
    flat = [value for group in groups for value in group]
    _, rows, width = flat[0].shape
    counts = tuple(group[0].shape[0] for group in groups)
    whole = sum(counts)
    pieces = whole // share
    outs = [packed_shape(share, rows, width)] * (pieces - keep_own)
    if keep_own:
        outs = [jax.ShapeDtypeStruct((share, rows, width), jnp.float32)] + outs
    arrivals = len(groups[0]) - 1
    return pl.pallas_call(
        functools.partial(combine_kernel, counts, arrivals, keep_own),
        out_shape=outs,
        grid_spec=pltpu.PrefetchScalarGridSpec(
            num_scalar_prefetch=1,
            grid=(),
            in_specs=[VMEM_SPEC] * len(flat),
            out_specs=[VMEM_SPEC] * len(outs),
            scratch_shapes=[
                pltpu.VMEM((whole, rows, width), jnp.float32),
                scale_scratch(share, rows, width),
            ]
            + [scale_scratch(max(counts), rows, width)] * arrivals,
        ),
        cost_estimate=TINY,
        compiler_params=PARAMS,
    )(targets, *flat)


def turn_kernel(column, *refs):
    *parts, out, whole, scales, tops = refs
    share = parts[0].shape[0] - extra_blocks_of(parts[0])
    columns = out.shape[0]
    groups = out.shape[1] - extra_blocks(whole.shape[0] // columns, out.shape[2])
    rows, width = out.shape[2:]
    for spot, part in enumerate(parts):
        load_scales(part, share, scales)

        def fill(index, part=part, spot=spot):
            whole[spot * share + index] = unpack_block(part[index], scales[pl.ds(index, 1), :])

        loop(share, fill)
    for group in range(groups):
        block = whole[group * columns : (group + 1) * columns].reshape(columns * rows, width).T
        for step in range(columns):
            whole[group * columns + step] = block[step * rows : (step + 1) * rows]
    for step in range(columns):
        target = column[0] ^ step

        def look(index, step=step):
            tops[pl.ds(index, 1), :] = top_of(whole[index * columns + step])

        loop(groups, look, unroll=2)
        store_scales(out.at[target], groups, tops)

        def put(index, step=step, target=target):
            block = whole[index * columns + step]
            out[target, index] = pack_block(block, tops[pl.ds(index, 1), :])

        loop(groups, put, unroll=2)


def turn(column, parts, share):
    columns = lax.axis_size("aux")
    _, rows, width = parts[0].shape
    whole = share * len(parts)
    one = packed_shape(whole // columns, rows, width)
    return pl.pallas_call(
        turn_kernel,
        out_shape=jax.ShapeDtypeStruct((columns,) + one.shape, one.dtype),
        grid_spec=pltpu.PrefetchScalarGridSpec(
            num_scalar_prefetch=1,
            grid=(),
            in_specs=[VMEM_SPEC] * len(parts),
            out_specs=VMEM_SPEC,
            scratch_shapes=[
                pltpu.VMEM((whole, rows, width), jnp.float32),
                scale_scratch(share, rows, width),
                scale_scratch(whole // columns, rows, width),
            ],
        ),
        cost_estimate=TINY,
        compiler_params=PARAMS,
    )(column.reshape(1), *parts)


def place_kernel(share, columns, kinds, sources, slots, *refs):
    *inputs, matrix, tiles, direct_scales, mirror_scales = refs
    directs, mirrors = inputs[: len(inputs) // 2], inputs[len(inputs) // 2 :]
    here, rows, _ = matrix.shape
    tile_count = kinds.shape[0] // here
    width = matrix.shape[2] // tile_count
    pack = width // rows
    chips = directs[0].shape[0]
    half = chips * share
    groups = half // pack
    lane = lax.broadcasted_iota(jnp.int32, (rows, width), 1) // rows
    for side in range(2):
        for chip in range(chips):
            load_scales(directs[side].at[chip], share, direct_scales.at[side, chip])
        for step in range(pack):
            load_scales(mirrors[side].at[step], groups, mirror_scales.at[side, step])

    def direct_of(source, write):
        for side in range(2):

            @pl.when(source // half == side)
            def _():
                inside = source - side * half
                chip = inside // share
                index = inside - chip * share
                write(
                    unpack_block(
                        directs[side][chip, index],
                        direct_scales[side, chip, pl.ds(index, 1), :],
                    )
                )

    for tile in range(here):

        def one(other, tile=tile):
            spot = tile * tile_count + other
            kind = kinds[spot]
            source = sources[spot]
            target = pl.ds(pl.multiple_of(other * width, width), width)

            def write(block):
                matrix[tile, :, target] = block

            @pl.when(kind == 0)
            def _():
                write(jnp.zeros((rows, width), jnp.float32))

            @pl.when(kind == 1)
            def _():
                direct_of(source, write)

            for side in range(2):

                @pl.when((kind == 2) & (source // half == side))
                def _():
                    inside = source - side * half
                    group = inside // pack
                    spot_in = inside - group * pack
                    total = jnp.zeros((rows, width), jnp.float32)
                    for step in range(pack):
                        column = columns[step]
                        block = unpack_block(
                            mirrors[side][step, group],
                            mirror_scales[side, step, pl.ds(group, 1), :],
                        )
                        moved = pltpu.roll(block, ((column - spot_in + pack) % pack) * rows, 1)
                        total = jnp.where(lane == column, moved, total)
                    write(total)

        loop(tile_count, one, unroll=1)

    def fill(slot):
        source = slots[slot]

        def write(block):
            tiles[0, slot] = block

        @pl.when(source < 0)
        def _():
            write(jnp.zeros((rows, width), jnp.float32))

        @pl.when(source >= 0)
        def _():
            direct_of(source, write)

    loop(tiles.shape[1], fill, unroll=1)


def place(columns, kinds, sources, slots, directs, mirrors, share, here, tile_count):
    chips, _, rows, width = directs[0].shape
    pack = mirrors[0].shape[0]
    groups = chips * share // pack
    return pl.pallas_call(
        functools.partial(place_kernel, share),
        out_shape=(
            jax.ShapeDtypeStruct((here, rows, tile_count * width), jnp.float32),
            jax.ShapeDtypeStruct((1, slots.shape[0], rows, width), jnp.float32),
        ),
        grid_spec=pltpu.PrefetchScalarGridSpec(
            num_scalar_prefetch=4,
            grid=(),
            in_specs=[VMEM_SPEC] * 4,
            out_specs=[VMEM_SPEC] * 2,
            scratch_shapes=[
                pltpu.VMEM((2, chips) + scale_scratch(share, rows, width).shape, jnp.float32),
                pltpu.VMEM((2, pack) + scale_scratch(groups, rows, width).shape, jnp.float32),
            ],
        ),
        cost_estimate=TINY,
        compiler_params=PARAMS,
    )(columns, kinds, sources, slots, *directs, *mirrors)


def take(value, index):
    return lax.dynamic_index_in_dim(value, index, 0, keepdims=False)


def body(factors, pairs, shared, owners):
    aux_rows, here, orbitals, width = factors.shape
    pair_size = lax.axis_size("pair")
    aux_size = lax.axis_size("aux")
    chips = pair_size // 2
    tile_count = here * pair_size
    pair_count = pairs.shape[0]
    rows = width // aux_size
    slot_count = 4 * (pair_count // pair_size)
    me = lax.axis_index("pair")
    core = me % 2
    chip = me // 2
    column = lax.axis_index("aux")
    depth = aux_rows // pair_size
    pack = aux_size
    unit = max(pack, chips)
    half = -(-(-(-pair_count // 2)) // unit) * unit
    share = half // chips
    padded = 2 * half

    pair_ids = jnp.arange(pair_count, dtype=jnp.int32)
    lefts, rights = pairs[:, 0], pairs[:, 1]
    same_owner = owners[:, None] == owners[None, :]
    rank = jnp.sum(
        (same_owner & (pair_ids[None, :] < pair_ids[:, None])).astype(jnp.int32), axis=1
    )
    tile_ids = jnp.arange(tile_count, dtype=jnp.int32)
    all_chips = jnp.arange(chips, dtype=jnp.int32)[:, None]
    steps_away = (tile_ids // (2 * here)) ^ all_chips
    is_last = (steps_away == chips - 1).astype(jnp.int32)
    group_of = is_last + is_last * (tile_ids % here == here - 1)
    left_hot = (lefts[:, None] == tile_ids).astype(jnp.int32)
    right_hot = (rights[:, None] == tile_ids).astype(jnp.int32)
    left_group = jnp.sum(left_hot[None] * group_of[:, None], axis=2)
    right_group = jnp.sum(right_hot[None] * group_of[:, None], axis=2)
    ready_at = jnp.maximum(left_group, right_group)
    arrival = ((tile_ids // here) ^ me) * here + tile_ids % here
    left_slots = jnp.sum(left_hot * arrival, axis=1)
    right_slots = jnp.sum(right_hot * arrival, axis=1)
    ready = take(ready_at, chip)

    real_half = -(-pair_count // 2)
    all_pairs = tile_count * (tile_count + 1) // 2
    bounds, enough = [0], jnp.bool_(True)
    stage_of = [here - 1]
    for stage in stage_of:
        known = tile_count - 2 * (here - stage)
        part = known * (known + 1) / 2 / all_pairs
        spread = (real_half * part * (1 - part) * (1 - real_half / all_pairs)) ** 0.5
        early = int(real_half * part - 3.75 * spread)
        bounds.append(early)
        ahead = (ready_at <= (stage if here > 1 else 0)).astype(jnp.int32)
        ahead = jnp.pad(ahead, ((0, 0), (0, padded - pair_count)))
        enough &= jnp.all(jnp.sum(ahead.reshape(chips, 2, half), axis=2) >= early)
    bounds.append(half)

    values = jnp.stack([left_slots, right_slots, shared[:, 0], ready])
    values = jnp.pad(values, ((0, 0), (0, padded - pair_count)))
    values = values.at[3, pair_count:].set(64) if padded > pair_count else values
    values = values.reshape(4, 2, half)
    local_ids = jnp.arange(half, dtype=jnp.int32)
    target_of = ((local_ids // share) ^ chip) * share + local_ids % share
    key = values[3] * half + local_ids
    spot_of = jnp.sum((key[:, None, :] < key[:, :, None]).astype(jnp.int32), axis=2)
    sorter = spot_of[:, None, :] == local_ids[:, None]
    fields = jnp.concatenate([values[:3], jnp.broadcast_to(target_of, (1, 2, half))])
    fields = jnp.sum(jnp.where(sorter[None], fields[:, :, None, :], 0), axis=3).astype(jnp.int32)
    mine = take(jnp.swapaxes(fields, 0, 1), core)
    theirs = take(jnp.swapaxes(fields, 0, 1), 1 - core)

    local = pair_ids % half
    part_core = pair_ids // half
    final_pos = (part_core ^ core) * half + ((local // share) ^ chip) * share + local % share
    my_rows = me * here + jnp.arange(here, dtype=jnp.int32)
    others = jnp.arange(tile_count, dtype=jnp.int32)
    is_direct = (lefts == my_rows[:, None, None]) & (rights == others[None, :, None])
    is_mirror = (rights == my_rows[:, None, None]) & (lefts == others[None, :, None])
    any_direct = jnp.any(is_direct, axis=-1)
    any_mirror = jnp.any(is_mirror, axis=-1)
    kinds = jnp.where(any_direct, 1, jnp.where(any_mirror, 2, 0)).astype(jnp.int32).reshape(-1)
    chosen = jnp.where(any_direct[..., None], is_direct, is_mirror)
    sources = jnp.sum(jnp.where(chosen, final_pos, 0), axis=-1).astype(jnp.int32).reshape(-1)
    slot_ids = jnp.arange(slot_count, dtype=jnp.int32)
    matches = (owners[None, :] == me) & (rank[None, :] == slot_ids[:, None])
    slots = jnp.sum(jnp.where(matches, final_pos + 1, 0), axis=1).astype(jnp.int32) - 1
    columns = column ^ jnp.arange(aux_size, dtype=jnp.int32)

    def piece(step, low, high, *earlier):
        source = lax.optimization_barrier((factors, earlier))[0] if earlier else factors
        start = ((me ^ step) * depth, low, 0, 0)
        return lax.dynamic_slice(source, start, (depth, high - low, orbitals, width))

    last = [pair_size - 2, pair_size - 1]
    far = [(step, 0, here) for step in range(pair_size - 3, 3, -1)]
    far += [(step, inner, inner + 1) for inner in range(here) for step in last]
    sent, order = {}, []
    for spot, (step, low, high) in enumerate(far):
        gate = order[spot - 2 : spot - 2 + 1] if spot >= 2 else ([first] if spot else [])
        block = piece(step, low, high, *gate)
        sent[step, low] = swap(block, "pair", pair_size, step)
        order.append(sent[step, low])
        if spot == 0:
            first = block
    for step in (3, 2, 1):
        sent[step, 0] = swap(piece(step, 0, here, first), "pair", pair_size, step)
    sent[0, 0] = piece(0, 0, here, first)
    parts = [
        [key for key in sent if key[0] not in last or key[1] < stage] for stage in stage_of
    ] + [list(sent)]

    def chip_blocks(keys, low, high, *earlier):
        given = [(step * here + inner, sent[step, inner]) for step, inner in keys]
        away = contract(given, theirs[:3, low:high], column, tile_count, aux_size, earlier)
        kept = contract(given, mine[:3, low:high], column, tile_count, aux_size, (away,))
        own, *others = split_columns(kept, swap(away, "pair", pair_size, 1))
        return [own] + [
            swap(other, "aux", aux_size, step + 1) for step, other in enumerate(others)
        ], kept

    groups, earlier = [], ()
    for keys, low, high in zip(parts, bounds[:-1], bounds[1:]):
        group, kept = chip_blocks(keys, low, high, *earlier)
        groups.append(group)
        earlier = (kept,)
    shares = combine(mine[3], groups, share, True)

    shares = lax.cond(
        enough,
        lambda: list(shares),
        lambda: list(combine(mine[3], [chip_blocks(list(sent), 0, half)[0]], share, True)),
    )

    line = [shares[0]] + [
        swap(shares[step], "pair", pair_size, 2 * step) for step in range(1, chips)
    ]
    total = combine(jnp.arange(share, dtype=jnp.int32), [line], share, False)[0]
    line = [total] + [swap(total, "pair", pair_size, 2 * step) for step in range(1, chips)]
    own_direct = jnp.stack(line)
    other_direct = swap(own_direct, "pair", pair_size, 1)

    turned = turn(column, line, share)
    own_mirror = jnp.stack(
        [turned[0]] + [swap(turned[step], "aux", aux_size, step) for step in range(1, aux_size)]
    )
    other_mirror = swap(own_mirror, "pair", pair_size, 1)
    return place(
        columns,
        kinds,
        sources,
        slots,
        (own_direct, other_direct),
        (own_mirror, other_mirror),
        share,
        here,
        tile_count,
    )


def solution(mesh):
    placed = (P("aux", "pair", None, None), P(), P(None, "aux"), P())
    return jax.shard_map(
        body,
        mesh=mesh,
        in_specs=placed,
        out_specs=(P("pair", "aux", None), P("pair", None, "aux", None)),
        check_vma=False,
    )
```

```python
import functools

import jax
import jax.numpy as jnp
from jax import lax
from jax.experimental import pallas as pl
from jax.experimental.pallas import tpu as pltpu
from jax.sharding import PartitionSpec as P

VMEM_LIMIT = 24 << 20
TINY = pl.CostEstimate(flops=1, transcendentals=0, bytes_accessed=1)


def swap(value, axis, size, step):
    return lax.ppermute(value, axis, [(i, i ^ step) for i in range(size)])


def contract_kernel(spots, table, *refs):
    *parts, out, tiles = refs
    parts = parts[: len(spots)]
    count = out.shape[1]
    rows = out.shape[2]
    length, width = tiles.shape[1:]
    column = table[3 * count]
    for spot, part in zip(spots, parts):
        for inner in range(part.shape[1]):
            tiles[spot + inner] = part[:, inner].reshape(length, width)

    def one(index, carry):
        block = lax.dot_general(
            tiles[table[index]],
            tiles[table[count + index]],
            (((0,), (0,)), ((), ())),
            preferred_element_type=jnp.float32,
        ) * table[2 * count + index].astype(jnp.float32)
        for step in range(out.shape[0]):
            out[column ^ step, index] = block[step * rows : (step + 1) * rows]
        return carry

    lax.fori_loop(0, count, one, 0, unroll=count if count <= 28 else 4)


def contract(parts, table, column, tile_count, aux_size, earlier):
    spots, values = zip(*parts)
    depth, _, orbitals, width = values[0].shape
    count = table.shape[1]
    return pl.pallas_call(
        functools.partial(contract_kernel, spots),
        out_shape=jax.ShapeDtypeStruct((aux_size, count, width // aux_size, width), jnp.float32),
        grid_spec=pltpu.PrefetchScalarGridSpec(
            num_scalar_prefetch=1,
            grid=(),
            in_specs=[pl.BlockSpec(memory_space=pltpu.VMEM)] * len(values)
            + [pl.BlockSpec(memory_space=pl.ANY)] * len(earlier),
            out_specs=pl.BlockSpec(memory_space=pltpu.VMEM),
            scratch_shapes=[pltpu.VMEM((tile_count, depth * orbitals, width), values[0].dtype)],
        ),
        cost_estimate=TINY,
        compiler_params=pltpu.CompilerParams(vmem_limit_bytes=VMEM_LIMIT),
    )(jnp.concatenate([table.reshape(-1), column.reshape(1)]), *values, *earlier)


LEVELS = 32766.0


def extra_blocks(count, rows):
    return -(-count // rows)


def packed_shape(count, rows, width):
    return jax.ShapeDtypeStruct((count + extra_blocks(count, rows), rows, width), jnp.int16)


def pack_block(block, factor):
    return jnp.round(block * factor).astype(jnp.int32).astype(jnp.int16)


def unpack_block(block, scale):
    return block.astype(jnp.int32).astype(jnp.float32) * scale


def load_scales(packed, count, scales):
    rows = packed.shape[1]
    for extra in range(extra_blocks(count, rows)):
        steps = packed[count + extra].astype(jnp.int32).astype(jnp.float32)
        scales[pl.ds(extra * rows, rows), :] = jnp.exp2(steps * (1 / 256)) * (1 / LEVELS)


def store_scales(packed, count, tops):
    rows = packed.shape[1]
    for extra in range(extra_blocks(count, rows)):
        here = pl.ds(extra * rows, rows)
        steps = jnp.ceil(jnp.log2(jnp.maximum(tops[here, :], 1e-30)) * 256) + 2
        packed[count + extra] = steps.astype(jnp.int32).astype(jnp.int16)
        tops[here, :] = jnp.exp2(steps * (-1 / 256)) * LEVELS


def top_of(block):
    return jnp.max(jnp.abs(block), axis=0, keepdims=True)


def loop(count, step, unroll=8):
    lax.fori_loop(0, count, lambda index, carry: (step(index), carry)[1], 0, unroll=unroll)


def split_kernel(kept, across, own, *refs):
    *outs, tops, total = refs
    count = own.shape[0]

    def keep(index):
        own[index] = kept[0, index] + across[0, index]

    loop(count, keep)
    for step, out in enumerate(outs):

        def add(index, step=step):
            block = kept[step + 1, index] + across[step + 1, index]
            total[index] = block
            tops[pl.ds(index, 1), :] = top_of(block)

        loop(count, add)
        store_scales(out, count, tops)

        def put(index, out=out):
            out[index] = pack_block(total[index], tops[pl.ds(index, 1), :])

        loop(count, put)


def scale_scratch(count, rows, width):
    return pltpu.VMEM((extra_blocks(count, rows) * rows, width), jnp.float32)


VMEM_SPEC = pl.BlockSpec(memory_space=pltpu.VMEM)
PARAMS = pltpu.CompilerParams(vmem_limit_bytes=VMEM_LIMIT)


def split_columns(kept, across):
    columns, count, rows, width = kept.shape
    return pl.pallas_call(
        split_kernel,
        out_shape=[jax.ShapeDtypeStruct((count, rows, width), jnp.float32)]
        + [packed_shape(count, rows, width)] * (columns - 1),
        in_specs=[VMEM_SPEC] * 2,
        out_specs=[VMEM_SPEC] * columns,
        scratch_shapes=[
            scale_scratch(count, rows, width),
            pltpu.VMEM((count, rows, width), jnp.float32),
        ],
        cost_estimate=TINY,
        compiler_params=PARAMS,
    )(kept, across)


def combine_kernel(counts, arrivals, keep_own, placed, *refs):
    targets = None
    if placed:
        targets, *refs = refs
    flat, refs = refs[: len(counts) * (arrivals + 1)], refs[len(counts) * (arrivals + 1) :]
    outs, (total, tops, *scales) = refs[: -2 - arrivals], refs[-2 - arrivals :]
    share = outs[-1].shape[0] - extra_blocks_of(outs[-1])
    base = 0
    for part, count in enumerate(counts):
        own, *others = flat[part * (arrivals + 1) : (part + 1) * (arrivals + 1)]
        for other, scale in zip(others, scales):
            load_scales(other, count, scale)

        def add(index, own=own, others=others, base=base):
            block = own[index]
            for other, scale in zip(others, scales):
                block = block + unpack_block(other[index], scale[pl.ds(index, 1), :])
            total[base + index if targets is None else targets[base + index]] = block

        loop(count, add)
        base += count
    packs = outs
    if keep_own:
        packs = outs[1:]

        def keep(index):
            outs[0][index] = total[index]

        loop(share, keep)
    for spot, out in enumerate(packs):
        start = (spot + 1) * share if keep_own else spot * share

        def look(index, start=start):
            tops[pl.ds(index, 1), :] = top_of(total[start + index])

        loop(share, look)
        store_scales(out, share, tops)

        def put(index, out=out, start=start):
            out[index] = pack_block(total[start + index], tops[pl.ds(index, 1), :])

        loop(share, put)


def extra_blocks_of(packed):
    blocks, rows = packed.shape[:2]
    count = next(n for n in range(blocks + 1) if n + extra_blocks(n, rows) == blocks)
    return blocks - count


def combine(targets, groups, share, keep_own):
    flat = [value for group in groups for value in group]
    _, rows, width = flat[0].shape
    counts = tuple(group[0].shape[0] for group in groups)
    whole = sum(counts)
    pieces = whole // share
    outs = [packed_shape(share, rows, width)] * (pieces - keep_own)
    if keep_own:
        outs = [jax.ShapeDtypeStruct((share, rows, width), jnp.float32)] + outs
    arrivals = len(groups[0]) - 1
    return pl.pallas_call(
        functools.partial(combine_kernel, counts, arrivals, keep_own, targets is not None),
        out_shape=outs,
        grid_spec=pltpu.PrefetchScalarGridSpec(
            num_scalar_prefetch=int(targets is not None),
            grid=(),
            in_specs=[VMEM_SPEC] * len(flat),
            out_specs=[VMEM_SPEC] * len(outs),
            scratch_shapes=[
                pltpu.VMEM((whole, rows, width), jnp.float32),
                scale_scratch(share, rows, width),
            ]
            + [scale_scratch(max(counts), rows, width)] * arrivals,
        ),
        cost_estimate=TINY,
        compiler_params=PARAMS,
    )(*([] if targets is None else [targets]), *flat)


def turn_kernel(column, *refs):
    *parts, out, whole, scales, tops = refs
    share = parts[0].shape[0] - extra_blocks_of(parts[0])
    columns = out.shape[0]
    groups = out.shape[1] - extra_blocks(whole.shape[0] // columns, out.shape[2])
    rows, width = out.shape[2:]
    for spot, part in enumerate(parts):
        load_scales(part, share, scales)

        def fill(index, part=part, spot=spot):
            whole[spot * share + index] = unpack_block(part[index], scales[pl.ds(index, 1), :])

        loop(share, fill)
    for group in range(groups):
        block = whole[group * columns : (group + 1) * columns].reshape(columns * rows, width).T
        for step in range(columns):
            whole[group * columns + step] = block[step * rows : (step + 1) * rows]
    for step in range(columns):
        target = column[0] ^ step

        def look(index, step=step):
            tops[pl.ds(index, 1), :] = top_of(whole[index * columns + step])

        loop(groups, look, unroll=2)
        store_scales(out.at[target], groups, tops)

        def put(index, step=step, target=target):
            block = whole[index * columns + step]
            out[target, index] = pack_block(block, tops[pl.ds(index, 1), :])

        loop(groups, put, unroll=2)


def turn(column, parts, share):
    columns = lax.axis_size("aux")
    _, rows, width = parts[0].shape
    whole = share * len(parts)
    one = packed_shape(whole // columns, rows, width)
    return pl.pallas_call(
        turn_kernel,
        out_shape=jax.ShapeDtypeStruct((columns,) + one.shape, one.dtype),
        grid_spec=pltpu.PrefetchScalarGridSpec(
            num_scalar_prefetch=1,
            grid=(),
            in_specs=[VMEM_SPEC] * len(parts),
            out_specs=VMEM_SPEC,
            scratch_shapes=[
                pltpu.VMEM((whole, rows, width), jnp.float32),
                scale_scratch(share, rows, width),
                scale_scratch(whole // columns, rows, width),
            ],
        ),
        cost_estimate=TINY,
        compiler_params=PARAMS,
    )(column.reshape(1), *parts)


def place_kernel(share, table, *refs):
    *inputs, matrix, tiles, direct_scales, mirror_scales = refs
    directs, mirrors = inputs[: len(inputs) // 2], inputs[len(inputs) // 2 :]
    here, rows, _ = matrix.shape
    width = directs[0].shape[-1]
    tile_count = matrix.shape[2] // width
    pack = width // rows
    spots = here * tile_count
    chips = directs[0].shape[0]
    half = chips * share
    groups = half // pack
    lane = lax.broadcasted_iota(jnp.int32, (rows, width), 1) // rows
    for side in range(2):
        for chip in range(chips):
            load_scales(directs[side].at[chip], share, direct_scales.at[side, chip])
        for step in range(pack):
            load_scales(mirrors[side].at[step], groups, mirror_scales.at[side, step])

    def direct_of(source, write):
        for side in range(2):

            @pl.when(source // half == side)
            def _():
                inside = source - side * half
                chip = inside // share
                index = inside - chip * share
                write(
                    unpack_block(
                        directs[side][chip, index],
                        direct_scales[side, chip, pl.ds(index, 1), :],
                    )
                )

    for tile in range(here):

        def one(other, tile=tile):
            spot = tile * tile_count + other
            kind = table[pack + spot]
            source = table[pack + spots + spot]
            target = pl.ds(pl.multiple_of(other * width, width), width)

            def write(block):
                matrix[tile, :, target] = block

            @pl.when(kind == 0)
            def _():
                write(jnp.zeros((rows, width), jnp.float32))

            @pl.when(kind == 1)
            def _():
                direct_of(source, write)

            for side in range(2):

                @pl.when((kind == 2) & (source // half == side))
                def _():
                    inside = source - side * half
                    group = inside // pack
                    spot_in = inside - group * pack
                    total = jnp.zeros((rows, width), jnp.float32)
                    for step in range(pack):
                        column = table[step]
                        block = unpack_block(
                            mirrors[side][step, group],
                            mirror_scales[side, step, pl.ds(group, 1), :],
                        )
                        moved = pltpu.roll(block, ((column - spot_in + pack) % pack) * rows, 1)
                        total = jnp.where(lane == column, moved, total)
                    write(total)

        loop(tile_count, one, unroll=1)

    def fill(slot):
        source = table[pack + 2 * spots + slot]

        def write(block):
            tiles[0, slot] = block

        @pl.when(source < 0)
        def _():
            write(jnp.zeros((rows, width), jnp.float32))

        @pl.when(source >= 0)
        def _():
            direct_of(source, write)

    loop(tiles.shape[1], fill, unroll=1)


def place(columns, kinds, sources, slots, directs, mirrors, share, here, tile_count):
    chips, _, rows, width = directs[0].shape
    pack = mirrors[0].shape[0]
    groups = chips * share // pack
    return pl.pallas_call(
        functools.partial(place_kernel, share),
        out_shape=(
            jax.ShapeDtypeStruct((here, rows, tile_count * width), jnp.float32),
            jax.ShapeDtypeStruct((1, slots.shape[0], rows, width), jnp.float32),
        ),
        grid_spec=pltpu.PrefetchScalarGridSpec(
            num_scalar_prefetch=1,
            grid=(),
            in_specs=[VMEM_SPEC] * 4,
            out_specs=[VMEM_SPEC] * 2,
            scratch_shapes=[
                pltpu.VMEM((2, chips) + scale_scratch(share, rows, width).shape, jnp.float32),
                pltpu.VMEM((2, pack) + scale_scratch(groups, rows, width).shape, jnp.float32),
            ],
        ),
        cost_estimate=TINY,
        compiler_params=PARAMS,
    )(jnp.concatenate([columns, kinds, sources, slots]), *directs, *mirrors)


def take(value, index):
    return lax.dynamic_index_in_dim(value, index, 0, keepdims=False)


def body(factors, pairs, shared, owners):
    aux_rows, here, orbitals, width = factors.shape
    pair_size = lax.axis_size("pair")
    aux_size = lax.axis_size("aux")
    chips = pair_size // 2
    tile_count = here * pair_size
    pair_count = pairs.shape[0]
    rows = width // aux_size
    slot_count = 4 * (pair_count // pair_size)
    me = lax.axis_index("pair")
    core = me % 2
    chip = me // 2
    column = lax.axis_index("aux")
    depth = aux_rows // pair_size
    pack = aux_size
    unit = max(pack, chips)
    half = -(-(-(-pair_count // 2)) // unit) * unit
    share = half // chips
    padded = 2 * half

    pair_ids = jnp.arange(pair_count, dtype=jnp.int32)
    lefts, rights = pairs[:, 0], pairs[:, 1]
    same_owner = owners[:, None] == owners[None, :]
    rank = jnp.sum(
        (same_owner & (pair_ids[None, :] < pair_ids[:, None])).astype(jnp.int32), axis=1
    )
    tile_ids = jnp.arange(tile_count, dtype=jnp.int32)
    all_chips = jnp.arange(chips, dtype=jnp.int32)[:, None]
    steps_away = (tile_ids // (2 * here)) ^ all_chips
    is_last = (steps_away == chips - 1).astype(jnp.int32)
    group_of = is_last + is_last * (tile_ids % here == here - 1)
    left_hot = (lefts[:, None] == tile_ids).astype(jnp.int32)
    right_hot = (rights[:, None] == tile_ids).astype(jnp.int32)
    left_group = jnp.sum(left_hot[None] * group_of[:, None], axis=2)
    right_group = jnp.sum(right_hot[None] * group_of[:, None], axis=2)
    ready_at = jnp.maximum(left_group, right_group)
    arrival = ((tile_ids // here) ^ me) * here + tile_ids % here
    left_slots = jnp.sum(left_hot * arrival, axis=1)
    right_slots = jnp.sum(right_hot * arrival, axis=1)
    ready = take(ready_at, chip)

    real_half = -(-pair_count // 2)
    all_pairs = tile_count * (tile_count + 1) // 2
    bounds, enough = [0], jnp.bool_(True)
    stage_of = [here - 1]
    for stage in stage_of:
        known = tile_count - 2 * (here - stage)
        part = known * (known + 1) / 2 / all_pairs
        spread = (real_half * part * (1 - part) * (1 - real_half / all_pairs)) ** 0.5
        early = int(real_half * part - 3.75 * spread)
        bounds.append(early)
        ahead = (ready_at <= (stage if here > 1 else 0)).astype(jnp.int32)
        ahead = jnp.pad(ahead, ((0, 0), (0, padded - pair_count)))
        enough &= jnp.all(jnp.sum(ahead.reshape(chips, 2, half), axis=2) >= early)
    bounds.append(half)

    values = jnp.stack([left_slots, right_slots, shared[:, 0], ready])
    values = jnp.pad(values, ((0, 0), (0, padded - pair_count)))
    values = values.at[3, pair_count:].set(64) if padded > pair_count else values
    values = values.reshape(4, 2, half)
    local_ids = jnp.arange(half, dtype=jnp.int32)
    target_of = ((local_ids // share) ^ chip) * share + local_ids % share
    key = values[3] * half + local_ids
    spot_of = jnp.sum((key[:, None, :] < key[:, :, None]).astype(jnp.int32), axis=2)
    sorter = spot_of[:, None, :] == local_ids[:, None]
    fields = jnp.concatenate([values[:3], jnp.broadcast_to(target_of, (1, 2, half))])
    fields = jnp.sum(jnp.where(sorter[None], fields[:, :, None, :], 0), axis=3).astype(jnp.int32)
    mine = take(jnp.swapaxes(fields, 0, 1), core)
    theirs = take(jnp.swapaxes(fields, 0, 1), 1 - core)

    local = pair_ids % half
    part_core = pair_ids // half
    final_pos = (part_core ^ core) * half + ((local // share) ^ chip) * share + local % share
    my_rows = me * here + jnp.arange(here, dtype=jnp.int32)
    others = jnp.arange(tile_count, dtype=jnp.int32)
    is_direct = (lefts == my_rows[:, None, None]) & (rights == others[None, :, None])
    is_mirror = (rights == my_rows[:, None, None]) & (lefts == others[None, :, None])
    any_direct = jnp.any(is_direct, axis=-1)
    any_mirror = jnp.any(is_mirror, axis=-1)
    kinds = jnp.where(any_direct, 1, jnp.where(any_mirror, 2, 0)).astype(jnp.int32).reshape(-1)
    chosen = jnp.where(any_direct[..., None], is_direct, is_mirror)
    sources = jnp.sum(jnp.where(chosen, final_pos, 0), axis=-1).astype(jnp.int32).reshape(-1)
    slot_ids = jnp.arange(slot_count, dtype=jnp.int32)
    matches = (owners[None, :] == me) & (rank[None, :] == slot_ids[:, None])
    slots = jnp.sum(jnp.where(matches, final_pos + 1, 0), axis=1).astype(jnp.int32) - 1
    columns = column ^ jnp.arange(aux_size, dtype=jnp.int32)

    def piece(step, low, high, *earlier):
        source = lax.optimization_barrier((factors, earlier))[0] if earlier else factors
        start = ((me ^ step) * depth, low, 0, 0)
        return lax.dynamic_slice(source, start, (depth, high - low, orbitals, width))

    last = [pair_size - 2, pair_size - 1]
    far = [(step, 0, here) for step in range(pair_size - 3, 3, -1)]
    far += [(step, inner, inner + 1) for inner in range(here) for step in last]
    sent, order = {}, []
    for spot, (step, low, high) in enumerate(far):
        gate = [order[spot - 2]] if spot >= 2 else ([first] if spot else [])
        block = piece(step, low, high, *gate)
        sent[step, low] = swap(block, "pair", pair_size, step)
        order.append(sent[step, low])
        if spot == 0:
            first = block
    for step in (3, 2, 1):
        sent[step, 0] = swap(piece(step, 0, here, first), "pair", pair_size, step)
    sent[0, 0] = piece(0, 0, here, first)
    parts = [
        [key for key in sent if key[0] not in last or key[1] < stage] for stage in stage_of
    ] + [list(sent)]

    def chip_blocks(keys, low, high, *earlier):
        given = [(step * here + inner, sent[step, inner]) for step, inner in keys]
        away = contract(given, theirs[:3, low:high], column, tile_count, aux_size, earlier)
        kept = contract(given, mine[:3, low:high], column, tile_count, aux_size, (away,))
        own, *others = split_columns(kept, swap(away, "pair", pair_size, 1))
        return [own] + [
            swap(other, "aux", aux_size, step + 1) for step, other in enumerate(others)
        ], kept

    groups, earlier = [], ()
    for keys, low, high in zip(parts, bounds[:-1], bounds[1:]):
        group, kept = chip_blocks(keys, low, high, *earlier)
        groups.append(group)
        earlier = (group[0],)
    shares = lax.cond(
        enough,
        lambda: list(combine(mine[3], groups, share, True)),
        lambda: list(combine(mine[3], [chip_blocks(list(sent), 0, half)[0]], share, True)),
    )

    line = [shares[0]] + [
        swap(shares[step], "pair", pair_size, 2 * step) for step in range(1, chips)
    ]
    total = combine(None, [line], share, False)[0]
    line = [total] + [swap(total, "pair", pair_size, 2 * step) for step in range(1, chips)]
    own_direct = jnp.stack(line)
    other_direct = swap(own_direct, "pair", pair_size, 1)

    turned = turn(column, line, share)
    own_mirror = jnp.stack(
        [turned[0]] + [swap(turned[step], "aux", aux_size, step) for step in range(1, aux_size)]
    )
    other_mirror = swap(own_mirror, "pair", pair_size, 1)
    return place(
        columns,
        kinds,
        sources,
        slots,
        (own_direct, other_direct),
        (own_mirror, other_mirror),
        share,
        here,
        tile_count,
    )


def solution(mesh):
    placed = (P("aux", "pair", None, None), P(), P(None, "aux"), P())
    return jax.shard_map(
        body,
        mesh=mesh,
        in_specs=placed,
        out_specs=(P("pair", "aux", None), P("pair", None, "aux", None)),
        check_vma=False,
    )
```

```python
import functools

import jax
import jax.numpy as jnp
from jax import lax
from jax.experimental import pallas as pl
from jax.experimental.pallas import tpu as pltpu
from jax.sharding import PartitionSpec as P

VMEM_LIMIT = 24 << 20
TINY = pl.CostEstimate(flops=1, transcendentals=0, bytes_accessed=1)


def swap(value, axis, size, step):
    return lax.ppermute(value, axis, [(i, i ^ step) for i in range(size)])


def contract_kernel(spots, table, *refs):
    *parts, out, tiles = refs
    parts = parts[: len(spots)]
    count = out.shape[1]
    rows = out.shape[2]
    length, width = tiles.shape[1:]
    column = table[3 * count]
    for spot, part in zip(spots, parts):
        for inner in range(part.shape[1]):
            tiles[spot + inner] = part[:, inner].reshape(length, width)

    def one(index, carry):
        block = lax.dot_general(
            tiles[table[index]],
            tiles[table[count + index]],
            (((0,), (0,)), ((), ())),
            preferred_element_type=jnp.float32,
        ) * table[2 * count + index].astype(jnp.float32)
        for step in range(out.shape[0]):
            out[column ^ step, index] = block[step * rows : (step + 1) * rows]
        return carry

    lax.fori_loop(0, count, one, 0, unroll=count if count <= 28 else 4)


def contract(parts, table, column, tile_count, aux_size, earlier):
    spots, values = zip(*parts)
    depth, _, orbitals, width = values[0].shape
    count = table.shape[1]
    return pl.pallas_call(
        functools.partial(contract_kernel, spots),
        out_shape=jax.ShapeDtypeStruct((aux_size, count, width // aux_size, width), jnp.float32),
        grid_spec=pltpu.PrefetchScalarGridSpec(
            num_scalar_prefetch=1,
            grid=(),
            in_specs=[pl.BlockSpec(memory_space=pltpu.VMEM)] * len(values)
            + [pl.BlockSpec(memory_space=pl.ANY)] * len(earlier),
            out_specs=pl.BlockSpec(memory_space=pltpu.VMEM),
            scratch_shapes=[pltpu.VMEM((tile_count, depth * orbitals, width), values[0].dtype)],
        ),
        cost_estimate=TINY,
        compiler_params=pltpu.CompilerParams(vmem_limit_bytes=VMEM_LIMIT),
    )(jnp.concatenate([table.reshape(-1), column.reshape(1)]), *values, *earlier)


LEVELS = 32766.0


def extra_blocks(count, rows):
    return -(-count // rows)


def packed_shape(count, rows, width):
    return jax.ShapeDtypeStruct((count + extra_blocks(count, rows), rows, width), jnp.int16)


def pack_block(block, factor):
    return jnp.round(block * factor).astype(jnp.int32).astype(jnp.int16)


def unpack_block(block, scale):
    return block.astype(jnp.int32).astype(jnp.float32) * scale


def load_scales(packed, count, scales):
    rows = packed.shape[1]
    for extra in range(extra_blocks(count, rows)):
        steps = packed[count + extra].astype(jnp.int32).astype(jnp.float32)
        scales[pl.ds(extra * rows, rows), :] = jnp.exp2(steps * (1 / 256)) * (1 / LEVELS)


def store_scales(packed, count, tops):
    rows = packed.shape[1]
    for extra in range(extra_blocks(count, rows)):
        here = pl.ds(extra * rows, rows)
        steps = jnp.ceil(jnp.log2(jnp.maximum(tops[here, :], 1e-30)) * 256) + 2
        packed[count + extra] = steps.astype(jnp.int32).astype(jnp.int16)
        tops[here, :] = jnp.exp2(steps * (-1 / 256)) * LEVELS


def top_of(block):
    return jnp.max(jnp.abs(block), axis=0, keepdims=True)


def loop(count, step, unroll=8):
    lax.fori_loop(0, count, lambda index, carry: (step(index), carry)[1], 0, unroll=unroll)


def split_kernel(kept, across, own, *refs):
    *outs, tops, total = refs
    count = own.shape[0]

    def keep(index):
        own[index] = kept[0, index] + across[0, index]

    loop(count, keep)
    for step, out in enumerate(outs):

        def add(index, step=step):
            block = kept[step + 1, index] + across[step + 1, index]
            total[index] = block
            tops[pl.ds(index, 1), :] = top_of(block)

        loop(count, add)
        store_scales(out, count, tops)

        def put(index, out=out):
            out[index] = pack_block(total[index], tops[pl.ds(index, 1), :])

        loop(count, put)


def scale_scratch(count, rows, width):
    return pltpu.VMEM((extra_blocks(count, rows) * rows, width), jnp.float32)


VMEM_SPEC = pl.BlockSpec(memory_space=pltpu.VMEM)
PARAMS = pltpu.CompilerParams(vmem_limit_bytes=VMEM_LIMIT)


def split_columns(kept, across):
    columns, count, rows, width = kept.shape
    return pl.pallas_call(
        split_kernel,
        out_shape=[jax.ShapeDtypeStruct((count, rows, width), jnp.float32)]
        + [packed_shape(count, rows, width)] * (columns - 1),
        in_specs=[VMEM_SPEC] * 2,
        out_specs=[VMEM_SPEC] * columns,
        scratch_shapes=[
            scale_scratch(count, rows, width),
            pltpu.VMEM((count, rows, width), jnp.float32),
        ],
        cost_estimate=TINY,
        compiler_params=PARAMS,
    )(kept, across)


def combine_kernel(counts, arrivals, keep_own, placed, *refs):
    targets = None
    if placed:
        targets, *refs = refs
    flat, refs = refs[: len(counts) * (arrivals + 1)], refs[len(counts) * (arrivals + 1) :]
    outs, (total, tops, *scales) = refs[: -2 - arrivals], refs[-2 - arrivals :]
    share = outs[-1].shape[0] - extra_blocks_of(outs[-1])
    base = 0
    for part, count in enumerate(counts):
        own, *others = flat[part * (arrivals + 1) : (part + 1) * (arrivals + 1)]
        for other, scale in zip(others, scales):
            load_scales(other, count, scale)

        def add(index, own=own, others=others, base=base):
            block = own[index]
            for other, scale in zip(others, scales):
                block = block + unpack_block(other[index], scale[pl.ds(index, 1), :])
            total[base + index if targets is None else targets[base + index]] = block

        loop(count, add)
        base += count
    packs = outs
    if keep_own:
        packs = outs[1:]

        def keep(index):
            outs[0][index] = total[index]

        loop(share, keep)
    for spot, out in enumerate(packs):
        start = (spot + 1) * share if keep_own else spot * share

        def look(index, start=start):
            tops[pl.ds(index, 1), :] = top_of(total[start + index])

        loop(share, look)
        store_scales(out, share, tops)

        def put(index, out=out, start=start):
            out[index] = pack_block(total[start + index], tops[pl.ds(index, 1), :])

        loop(share, put)


def extra_blocks_of(packed):
    blocks, rows = packed.shape[:2]
    count = next(n for n in range(blocks + 1) if n + extra_blocks(n, rows) == blocks)
    return blocks - count


def combine(targets, groups, share, keep_own):
    flat = [value for group in groups for value in group]
    _, rows, width = flat[0].shape
    counts = tuple(group[0].shape[0] for group in groups)
    whole = sum(counts)
    pieces = whole // share
    outs = [packed_shape(share, rows, width)] * (pieces - keep_own)
    if keep_own:
        outs = [jax.ShapeDtypeStruct((share, rows, width), jnp.float32)] + outs
    arrivals = len(groups[0]) - 1
    return pl.pallas_call(
        functools.partial(combine_kernel, counts, arrivals, keep_own, targets is not None),
        out_shape=outs,
        grid_spec=pltpu.PrefetchScalarGridSpec(
            num_scalar_prefetch=int(targets is not None),
            grid=(),
            in_specs=[VMEM_SPEC] * len(flat),
            out_specs=[VMEM_SPEC] * len(outs),
            scratch_shapes=[
                pltpu.VMEM((whole, rows, width), jnp.float32),
                scale_scratch(share, rows, width),
            ]
            + [scale_scratch(max(counts), rows, width)] * arrivals,
        ),
        cost_estimate=TINY,
        compiler_params=PARAMS,
    )(*([] if targets is None else [targets]), *flat)


def turn_kernel(column, *refs):
    *parts, out, whole, scales, tops = refs
    share = parts[0].shape[0] - extra_blocks_of(parts[0])
    columns = out.shape[0]
    groups = out.shape[1] - extra_blocks(whole.shape[0] // columns, out.shape[2])
    rows, width = out.shape[2:]
    for spot, part in enumerate(parts):
        load_scales(part, share, scales)

        def fill(index, part=part, spot=spot):
            whole[spot * share + index] = unpack_block(part[index], scales[pl.ds(index, 1), :])

        loop(share, fill)
    for group in range(groups):
        block = whole[group * columns : (group + 1) * columns].reshape(columns * rows, width).T
        for step in range(columns):
            whole[group * columns + step] = block[step * rows : (step + 1) * rows]
    for step in range(columns):
        target = column[0] ^ step

        def look(index, step=step):
            tops[pl.ds(index, 1), :] = top_of(whole[index * columns + step])

        loop(groups, look, unroll=2)
        store_scales(out.at[target], groups, tops)

        def put(index, step=step, target=target):
            block = whole[index * columns + step]
            out[target, index] = pack_block(block, tops[pl.ds(index, 1), :])

        loop(groups, put, unroll=2)


def turn(column, parts, share):
    columns = lax.axis_size("aux")
    _, rows, width = parts[0].shape
    whole = share * len(parts)
    one = packed_shape(whole // columns, rows, width)
    return pl.pallas_call(
        turn_kernel,
        out_shape=jax.ShapeDtypeStruct((columns,) + one.shape, one.dtype),
        grid_spec=pltpu.PrefetchScalarGridSpec(
            num_scalar_prefetch=1,
            grid=(),
            in_specs=[VMEM_SPEC] * len(parts),
            out_specs=VMEM_SPEC,
            scratch_shapes=[
                pltpu.VMEM((whole, rows, width), jnp.float32),
                scale_scratch(share, rows, width),
                scale_scratch(whole // columns, rows, width),
            ],
        ),
        cost_estimate=TINY,
        compiler_params=PARAMS,
    )(column.reshape(1), *parts)


def place_kernel(share, chips, table, *refs):
    direct, *mirrors, matrix, tiles, direct_scales, mirror_scales = refs
    here, rows, _ = matrix.shape
    width = direct.shape[-1]
    tile_count = matrix.shape[2] // width
    pack = width // rows
    spots = here * tile_count
    slots = tiles.shape[1]
    half = chips * share
    groups = half // pack
    blocks = share + extra_blocks(share, rows)
    behind = extra_blocks(share, rows) * rows
    for chip in range(2 * chips):
        load_scales(
            direct.at[pl.ds(chip * blocks, blocks)],
            share,
            direct_scales.at[pl.ds(chip * behind, behind)],
        )
    direct_scales[pl.ds(2 * chips * behind, rows), :] = jnp.zeros((rows, width), jnp.float32)
    for side in range(2):
        for step in range(pack):
            load_scales(mirrors[side].at[step], groups, mirror_scales.at[side, step])

    def direct_block(spot):
        scale = direct_scales[pl.ds(table[spots + slots + spot], 1), :]
        return unpack_block(direct[table[spot]], scale)

    for tile in range(here):

        def one(other, tile=tile):
            target = pl.ds(pl.multiple_of(other * width, width), width)
            matrix[tile, :, target] = direct_block(tile * tile_count + other)

        loop(tile_count, one)

    def fill(slot):
        tiles[0, slot] = direct_block(spots + slot)

    loop(slots, fill)

    lane = lax.broadcasted_iota(jnp.int32, (rows, width), 1) // rows
    base = 2 * (spots + slots)

    def transposed(item, carry):
        spot = table[base + 1 + item]
        source = table[base + 1 + spots + item]
        for side in range(2):

            @pl.when(source // half == side)
            def _():
                inside = source - side * half
                group = inside // pack
                spot_in = inside - group * pack
                total = jnp.zeros((rows, width), jnp.float32)
                for step in range(pack):
                    column = table[base + 1 + 2 * spots + step]
                    scale = mirror_scales[side, step, pl.ds(group, 1), :]
                    block = unpack_block(mirrors[side][step, group], scale)
                    moved = pltpu.roll(block, ((column - spot_in + pack) % pack) * rows, 1)
                    total = jnp.where(lane == column, moved, total)
                tile = spot // tile_count
                other = spot - tile * tile_count
                target = pl.ds(pl.multiple_of(other * width, width), width)
                matrix[tile, :, target] = total

        return carry

    lax.fori_loop(0, table[base], transposed, 0)


def place_table(columns, kinds, sources, slots, share, chips, rows):
    blocks = share + extra_blocks(share, rows)
    behind = extra_blocks(share, rows) * rows
    spots = kinds.shape[0]
    wanted = jnp.concatenate([jnp.where(kinds == 1, sources, -1), slots])
    there = wanted >= 0
    chip = wanted // share
    inside = wanted % share
    block_at = jnp.where(there, chip * blocks + inside, 0)
    scale_at = jnp.where(there, chip * behind + inside, 2 * chips * behind)
    turned = kinds == 2
    spot_ids = jnp.arange(spots, dtype=jnp.int32)
    rank = jnp.sum((turned[None, :] & (spot_ids[None, :] < spot_ids[:, None])), axis=1)
    hot = turned[None, :] & (rank[None, :] == spot_ids[:, None])
    listed = jnp.sum(jnp.where(hot[None], jnp.stack([spot_ids, sources])[:, None], 0), axis=2)
    count = jnp.sum(turned.astype(jnp.int32)).reshape(1)
    table = jnp.concatenate([block_at, scale_at, count, listed.reshape(-1), columns])
    return table.astype(jnp.int32)


def place(table, directs, mirrors, share, here, tile_count, slot_count):
    chips, blocks, rows, width = directs[0].shape
    pack = mirrors[0].shape[0]
    groups = chips * share // pack
    behind = extra_blocks(share, rows) * rows
    direct = jnp.concatenate(directs, axis=0).reshape(2 * chips * blocks, rows, width)
    return pl.pallas_call(
        functools.partial(place_kernel, share, chips),
        out_shape=(
            jax.ShapeDtypeStruct((here, rows, tile_count * width), jnp.float32),
            jax.ShapeDtypeStruct((1, slot_count, rows, width), jnp.float32),
        ),
        grid_spec=pltpu.PrefetchScalarGridSpec(
            num_scalar_prefetch=1,
            grid=(),
            in_specs=[VMEM_SPEC] * 3,
            out_specs=[VMEM_SPEC] * 2,
            scratch_shapes=[
                pltpu.VMEM((2 * chips * behind + rows, width), jnp.float32),
                pltpu.VMEM((2, pack) + scale_scratch(groups, rows, width).shape, jnp.float32),
            ],
        ),
        cost_estimate=TINY,
        compiler_params=PARAMS,
    )(table, direct, *mirrors)


def take(value, index):
    return lax.dynamic_index_in_dim(value, index, 0, keepdims=False)


def body(factors, pairs, shared, owners):
    aux_rows, here, orbitals, width = factors.shape
    pair_size = lax.axis_size("pair")
    aux_size = lax.axis_size("aux")
    chips = pair_size // 2
    tile_count = here * pair_size
    pair_count = pairs.shape[0]
    rows = width // aux_size
    slot_count = 4 * (pair_count // pair_size)
    me = lax.axis_index("pair")
    core = me % 2
    chip = me // 2
    column = lax.axis_index("aux")
    depth = aux_rows // pair_size
    pack = aux_size
    unit = max(pack, chips)
    half = -(-(-(-pair_count // 2)) // unit) * unit
    share = half // chips
    padded = 2 * half

    pair_ids = jnp.arange(pair_count, dtype=jnp.int32)
    lefts, rights = pairs[:, 0], pairs[:, 1]
    same_owner = owners[:, None] == owners[None, :]
    rank = jnp.sum(
        (same_owner & (pair_ids[None, :] < pair_ids[:, None])).astype(jnp.int32), axis=1
    )
    tile_ids = jnp.arange(tile_count, dtype=jnp.int32)
    all_chips = jnp.arange(chips, dtype=jnp.int32)[:, None]
    steps_away = (tile_ids // (2 * here)) ^ all_chips
    is_last = (steps_away == chips - 1).astype(jnp.int32)
    group_of = is_last + is_last * (tile_ids % here == here - 1)
    left_hot = (lefts[:, None] == tile_ids).astype(jnp.int32)
    right_hot = (rights[:, None] == tile_ids).astype(jnp.int32)
    left_group = jnp.sum(left_hot[None] * group_of[:, None], axis=2)
    right_group = jnp.sum(right_hot[None] * group_of[:, None], axis=2)
    ready_at = jnp.maximum(left_group, right_group)
    arrival = ((tile_ids // here) ^ me) * here + tile_ids % here
    left_slots = jnp.sum(left_hot * arrival, axis=1)
    right_slots = jnp.sum(right_hot * arrival, axis=1)
    ready = take(ready_at, chip)

    real_half = -(-pair_count // 2)
    all_pairs = tile_count * (tile_count + 1) // 2
    bounds, enough = [0], jnp.bool_(True)
    stage_of = [here - 1]
    for stage in stage_of:
        known = tile_count - 2 * (here - stage)
        part = known * (known + 1) / 2 / all_pairs
        spread = (real_half * part * (1 - part) * (1 - real_half / all_pairs)) ** 0.5
        early = int(real_half * part - 3.75 * spread)
        bounds.append(early)
        ahead = (ready_at <= (stage if here > 1 else 0)).astype(jnp.int32)
        ahead = jnp.pad(ahead, ((0, 0), (0, padded - pair_count)))
        enough &= jnp.all(jnp.sum(ahead.reshape(chips, 2, half), axis=2) >= early)
    bounds.append(half)

    values = jnp.stack([left_slots, right_slots, shared[:, 0], ready])
    values = jnp.pad(values, ((0, 0), (0, padded - pair_count)))
    values = values.at[3, pair_count:].set(64) if padded > pair_count else values
    values = values.reshape(4, 2, half)
    local_ids = jnp.arange(half, dtype=jnp.int32)
    target_of = ((local_ids // share) ^ chip) * share + local_ids % share
    key = values[3] * half + local_ids
    spot_of = jnp.sum((key[:, None, :] < key[:, :, None]).astype(jnp.int32), axis=2)
    sorter = spot_of[:, None, :] == local_ids[:, None]
    fields = jnp.concatenate([values[:3], jnp.broadcast_to(target_of, (1, 2, half))])
    fields = jnp.sum(jnp.where(sorter[None], fields[:, :, None, :], 0), axis=3).astype(jnp.int32)
    mine = take(jnp.swapaxes(fields, 0, 1), core)
    theirs = take(jnp.swapaxes(fields, 0, 1), 1 - core)

    local = pair_ids % half
    part_core = pair_ids // half
    final_pos = (part_core ^ core) * half + ((local // share) ^ chip) * share + local % share
    my_rows = me * here + jnp.arange(here, dtype=jnp.int32)
    others = jnp.arange(tile_count, dtype=jnp.int32)
    is_direct = (lefts == my_rows[:, None, None]) & (rights == others[None, :, None])
    is_mirror = (rights == my_rows[:, None, None]) & (lefts == others[None, :, None])
    any_direct = jnp.any(is_direct, axis=-1)
    any_mirror = jnp.any(is_mirror, axis=-1)
    kinds = jnp.where(any_direct, 1, jnp.where(any_mirror, 2, 0)).astype(jnp.int32).reshape(-1)
    chosen = jnp.where(any_direct[..., None], is_direct, is_mirror)
    sources = jnp.sum(jnp.where(chosen, final_pos, 0), axis=-1).astype(jnp.int32).reshape(-1)
    slot_ids = jnp.arange(slot_count, dtype=jnp.int32)
    matches = (owners[None, :] == me) & (rank[None, :] == slot_ids[:, None])
    slots = jnp.sum(jnp.where(matches, final_pos + 1, 0), axis=1).astype(jnp.int32) - 1
    columns = column ^ jnp.arange(aux_size, dtype=jnp.int32)
    table = place_table(columns, kinds, sources, slots, share, chips, rows)

    def piece(step, low, high, *earlier):
        source = lax.optimization_barrier((factors, earlier))[0] if earlier else factors
        start = ((me ^ step) * depth, low, 0, 0)
        return lax.dynamic_slice(source, start, (depth, high - low, orbitals, width))

    last = [pair_size - 2, pair_size - 1]
    far = [(step, 0, here) for step in range(pair_size - 3, 3, -1)]
    far += [(step, inner, inner + 1) for inner in range(here) for step in last]
    sent, order = {}, []
    for spot, (step, low, high) in enumerate(far):
        gate = [order[max(0, spot - 4) if spot > 3 else 0]] if spot >= 2 else [first] if spot else []
        block = piece(step, low, high, *gate)
        sent[step, low] = swap(block, "pair", pair_size, step)
        order.append(sent[step, low])
        if spot == 0:
            first = block
    for step in (3, 2, 1):
        sent[step, 0] = swap(piece(step, 0, here, first), "pair", pair_size, step)
    sent[0, 0] = piece(0, 0, here, first)
    parts = [
        [key for key in sent if key[0] not in last or key[1] < stage] for stage in stage_of
    ] + [list(sent)]

    def chip_blocks(keys, low, high, *earlier):
        given = [(step * here + inner, sent[step, inner]) for step, inner in keys]
        away = contract(given, theirs[:3, low:high], column, tile_count, aux_size, earlier)
        kept = contract(given, mine[:3, low:high], column, tile_count, aux_size, (away,))
        own, *others = split_columns(kept, swap(away, "pair", pair_size, 1))
        return [own] + [
            swap(other, "aux", aux_size, step + 1) for step, other in enumerate(others)
        ], kept

    groups, earlier = [], (table, mine, theirs, enough.astype(jnp.int32).reshape(1))
    for keys, low, high in zip(parts, bounds[:-1], bounds[1:]):
        group, kept = chip_blocks(keys, low, high, *earlier)
        groups.append(group)
        earlier = (group[0],)
    shares = lax.cond(
        enough,
        lambda: list(combine(mine[3], groups, share, True)),
        lambda: list(combine(mine[3], [chip_blocks(list(sent), 0, half)[0]], share, True)),
    )

    line = [shares[0]] + [
        swap(shares[step], "pair", pair_size, 2 * step) for step in range(1, chips)
    ]
    total = combine(None, [line], share, False)[0]
    line = [total] + [swap(total, "pair", pair_size, 2 * step) for step in range(1, chips)]
    own_direct = jnp.stack(line)
    other_direct = swap(own_direct, "pair", pair_size, 1)

    turned = turn(column, line, share)
    own_mirror = jnp.stack(
        [turned[0]] + [swap(turned[step], "aux", aux_size, step) for step in range(1, aux_size)]
    )
    other_mirror = swap(own_mirror, "pair", pair_size, 1)
    directs, mirrors = (own_direct, other_direct), (own_mirror, other_mirror)
    return place(table, directs, mirrors, share, here, tile_count, slot_count)


def solution(mesh):
    placed = (P("aux", "pair", None, None), P(), P(None, "aux"), P())
    return jax.shard_map(
        body,
        mesh=mesh,
        in_specs=placed,
        out_specs=(P("pair", "aux", None), P("pair", None, "aux", None)),
        check_vma=False,
    )
```

```python
import functools

import jax
import jax.numpy as jnp
from jax import lax
from jax.experimental import pallas as pl
from jax.experimental.pallas import tpu as pltpu
from jax.sharding import PartitionSpec as P

VMEM_LIMIT = 24 << 20
TINY = pl.CostEstimate(flops=1, transcendentals=0, bytes_accessed=1)


def swap(value, axis, size, step):
    return lax.ppermute(value, axis, [(i, i ^ step) for i in range(size)])


def contract_kernel(spots, table, *refs):
    *parts, out, tiles = refs
    parts = parts[: len(spots)]
    count = out.shape[1]
    rows = out.shape[2]
    length, width = tiles.shape[1:]
    column = table[3 * count]
    for spot, part in zip(spots, parts):
        for inner in range(part.shape[1]):
            tiles[spot + inner] = part[:, inner].reshape(length, width)

    def one(index, carry):
        block = lax.dot_general(
            tiles[table[index]],
            tiles[table[count + index]],
            (((0,), (0,)), ((), ())),
            preferred_element_type=jnp.float32,
        ) * table[2 * count + index].astype(jnp.float32)
        for step in range(out.shape[0]):
            out[column ^ step, index] = block[step * rows : (step + 1) * rows]
        return carry

    lax.fori_loop(0, count, one, 0, unroll=count if count <= 28 else 4)


def contract(parts, table, column, tile_count, aux_size, earlier):
    spots, values = zip(*parts)
    depth, _, orbitals, width = values[0].shape
    count = table.shape[1]
    return pl.pallas_call(
        functools.partial(contract_kernel, spots),
        out_shape=jax.ShapeDtypeStruct((aux_size, count, width // aux_size, width), jnp.float32),
        grid_spec=pltpu.PrefetchScalarGridSpec(
            num_scalar_prefetch=1,
            grid=(),
            in_specs=[pl.BlockSpec(memory_space=pltpu.VMEM)] * len(values)
            + [pl.BlockSpec(memory_space=pl.ANY)] * len(earlier),
            out_specs=pl.BlockSpec(memory_space=pltpu.VMEM),
            scratch_shapes=[pltpu.VMEM((tile_count, depth * orbitals, width), values[0].dtype)],
        ),
        cost_estimate=TINY,
        compiler_params=pltpu.CompilerParams(vmem_limit_bytes=VMEM_LIMIT),
    )(jnp.concatenate([table.reshape(-1), column.reshape(1)]), *values, *earlier)


LEVELS = 32766.0


def extra_blocks(count, rows):
    return -(-count // rows)


def packed_shape(count, rows, width):
    return jax.ShapeDtypeStruct((count + extra_blocks(count, rows), rows, width), jnp.int16)


def pack_block(block, factor):
    return jnp.round(block * factor).astype(jnp.int32).astype(jnp.int16)


def unpack_block(block, scale):
    return block.astype(jnp.int32).astype(jnp.float32) * scale


def load_scales(packed, count, scales):
    rows = packed.shape[1]
    for extra in range(extra_blocks(count, rows)):
        steps = packed[count + extra].astype(jnp.int32).astype(jnp.float32)
        scales[pl.ds(extra * rows, rows), :] = jnp.exp2(steps * (1 / 256)) * (1 / LEVELS)


def store_scales(packed, count, tops):
    rows = packed.shape[1]
    for extra in range(extra_blocks(count, rows)):
        here = pl.ds(extra * rows, rows)
        steps = jnp.ceil(jnp.log2(jnp.maximum(tops[here, :], 1e-30)) * 256) + 2
        packed[count + extra] = steps.astype(jnp.int32).astype(jnp.int16)
        tops[here, :] = jnp.exp2(steps * (-1 / 256)) * LEVELS


def top_of(block):
    return jnp.max(jnp.abs(block), axis=0, keepdims=True)


def loop(count, step, unroll=8):
    lax.fori_loop(0, count, lambda index, carry: (step(index), carry)[1], 0, unroll=unroll)


def split_kernel(kept, across, own, *refs):
    *outs, tops, total = refs
    count = own.shape[0]

    def keep(index):
        own[index] = kept[0, index] + across[0, index]

    loop(count, keep)
    for step, out in enumerate(outs):

        def add(index, step=step):
            block = kept[step + 1, index] + across[step + 1, index]
            total[index] = block
            tops[pl.ds(index, 1), :] = top_of(block)

        loop(count, add)
        store_scales(out, count, tops)

        def put(index, out=out):
            out[index] = pack_block(total[index], tops[pl.ds(index, 1), :])

        loop(count, put)


def scale_scratch(count, rows, width):
    return pltpu.VMEM((extra_blocks(count, rows) * rows, width), jnp.float32)


VMEM_SPEC = pl.BlockSpec(memory_space=pltpu.VMEM)
PARAMS = pltpu.CompilerParams(vmem_limit_bytes=VMEM_LIMIT)


def split_columns(kept, across):
    columns, count, rows, width = kept.shape
    return pl.pallas_call(
        split_kernel,
        out_shape=[jax.ShapeDtypeStruct((count, rows, width), jnp.float32)]
        + [packed_shape(count, rows, width)] * (columns - 1),
        in_specs=[VMEM_SPEC] * 2,
        out_specs=[VMEM_SPEC] * columns,
        scratch_shapes=[
            scale_scratch(count, rows, width),
            pltpu.VMEM((count, rows, width), jnp.float32),
        ],
        cost_estimate=TINY,
        compiler_params=PARAMS,
    )(kept, across)


def combine_kernel(counts, arrivals, keep_own, placed, *refs):
    targets = None
    if placed:
        targets, *refs = refs
    flat, refs = refs[: len(counts) * (arrivals + 1)], refs[len(counts) * (arrivals + 1) :]
    outs, (total, tops, *scales) = refs[: -2 - arrivals], refs[-2 - arrivals :]
    share = outs[-1].shape[0] - extra_blocks_of(outs[-1])
    base = 0
    for part, count in enumerate(counts):
        own, *others = flat[part * (arrivals + 1) : (part + 1) * (arrivals + 1)]
        for other, scale in zip(others, scales):
            load_scales(other, count, scale)

        def add(index, own=own, others=others, base=base):
            block = own[index]
            for other, scale in zip(others, scales):
                block = block + unpack_block(other[index], scale[pl.ds(index, 1), :])
            total[base + index if targets is None else targets[base + index]] = block

        loop(count, add)
        base += count
    packs = outs
    if keep_own:
        packs = outs[1:]

        def keep(index):
            outs[0][index] = total[index]

        loop(share, keep)
    for spot, out in enumerate(packs):
        start = (spot + 1) * share if keep_own else spot * share

        def look(index, start=start):
            tops[pl.ds(index, 1), :] = top_of(total[start + index])

        loop(share, look)
        store_scales(out, share, tops)

        def put(index, out=out, start=start):
            out[index] = pack_block(total[start + index], tops[pl.ds(index, 1), :])

        loop(share, put)


def extra_blocks_of(packed):
    blocks, rows = packed.shape[:2]
    count = next(n for n in range(blocks + 1) if n + extra_blocks(n, rows) == blocks)
    return blocks - count


def combine(targets, groups, share, keep_own):
    flat = [value for group in groups for value in group]
    _, rows, width = flat[0].shape
    counts = tuple(group[0].shape[0] for group in groups)
    whole = sum(counts)
    pieces = whole // share
    outs = [packed_shape(share, rows, width)] * (pieces - keep_own)
    if keep_own:
        outs = [jax.ShapeDtypeStruct((share, rows, width), jnp.float32)] + outs
    arrivals = len(groups[0]) - 1
    return pl.pallas_call(
        functools.partial(combine_kernel, counts, arrivals, keep_own, targets is not None),
        out_shape=outs,
        grid_spec=pltpu.PrefetchScalarGridSpec(
            num_scalar_prefetch=int(targets is not None),
            grid=(),
            in_specs=[VMEM_SPEC] * len(flat),
            out_specs=[VMEM_SPEC] * len(outs),
            scratch_shapes=[
                pltpu.VMEM((whole, rows, width), jnp.float32),
                scale_scratch(share, rows, width),
            ]
            + [scale_scratch(max(counts), rows, width)] * arrivals,
        ),
        cost_estimate=TINY,
        compiler_params=PARAMS,
    )(*([] if targets is None else [targets]), *flat)


def turn_kernel(column, *refs):
    *parts, out, whole, scales, tops = refs
    share = parts[0].shape[0] - extra_blocks_of(parts[0])
    columns = out.shape[0]
    groups = out.shape[1] - extra_blocks(whole.shape[0] // columns, out.shape[2])
    rows, width = out.shape[2:]
    for spot, part in enumerate(parts):
        load_scales(part, share, scales)

        def fill(index, part=part, spot=spot):
            whole[spot * share + index] = unpack_block(part[index], scales[pl.ds(index, 1), :])

        loop(share, fill)
    for group in range(groups):
        block = whole[group * columns : (group + 1) * columns].reshape(columns * rows, width).T
        for step in range(columns):
            whole[group * columns + step] = block[step * rows : (step + 1) * rows]
    for step in range(columns):
        target = column[0] ^ step

        def look(index, step=step):
            tops[pl.ds(index, 1), :] = top_of(whole[index * columns + step])

        loop(groups, look, unroll=2)
        store_scales(out.at[target], groups, tops)

        def put(index, step=step, target=target):
            block = whole[index * columns + step]
            out[target, index] = pack_block(block, tops[pl.ds(index, 1), :])

        loop(groups, put, unroll=2)


def turn(column, parts, share):
    columns = lax.axis_size("aux")
    _, rows, width = parts[0].shape
    whole = share * len(parts)
    one = packed_shape(whole // columns, rows, width)
    return pl.pallas_call(
        turn_kernel,
        out_shape=jax.ShapeDtypeStruct((columns,) + one.shape, one.dtype),
        grid_spec=pltpu.PrefetchScalarGridSpec(
            num_scalar_prefetch=1,
            grid=(),
            in_specs=[VMEM_SPEC] * len(parts),
            out_specs=VMEM_SPEC,
            scratch_shapes=[
                pltpu.VMEM((whole, rows, width), jnp.float32),
                scale_scratch(share, rows, width),
                scale_scratch(whole // columns, rows, width),
            ],
        ),
        cost_estimate=TINY,
        compiler_params=PARAMS,
    )(column.reshape(1), *parts)


def place_kernel(share, chips, table, *refs):
    direct, *mirrors, matrix, tiles, direct_scales, mirror_scales = refs
    here, rows, _ = matrix.shape
    width = direct.shape[-1]
    tile_count = matrix.shape[2] // width
    pack = width // rows
    spots = here * tile_count
    slots = tiles.shape[1]
    half = chips * share
    groups = half // pack
    blocks = share + extra_blocks(share, rows)
    behind = extra_blocks(share, rows) * rows
    for chip in range(2 * chips):
        load_scales(
            direct.at[pl.ds(chip * blocks, blocks)],
            share,
            direct_scales.at[pl.ds(chip * behind, behind)],
        )
    direct_scales[pl.ds(2 * chips * behind, rows), :] = jnp.zeros((rows, width), jnp.float32)
    for side in range(2):
        for step in range(pack):
            load_scales(mirrors[side].at[step], groups, mirror_scales.at[side, step])

    def direct_block(spot):
        scale = direct_scales[pl.ds(table[spots + slots + spot], 1), :]
        return unpack_block(direct[table[spot]], scale)

    for tile in range(here):

        def one(other, tile=tile):
            target = pl.ds(pl.multiple_of(other * width, width), width)
            matrix[tile, :, target] = direct_block(tile * tile_count + other)

        loop(tile_count, one)

    def fill(slot):
        tiles[0, slot] = direct_block(spots + slot)

    loop(slots, fill)

    lane = lax.broadcasted_iota(jnp.int32, (rows, width), 1) // rows
    base = 2 * (spots + slots)

    def transposed(item, carry):
        spot = table[base + 1 + item]
        source = table[base + 1 + spots + item]
        for side in range(2):

            @pl.when(source // half == side)
            def _():
                inside = source - side * half
                group = inside // pack
                spot_in = inside - group * pack
                total = jnp.zeros((rows, width), jnp.float32)
                for step in range(pack):
                    column = table[base + 1 + 2 * spots + step]
                    scale = mirror_scales[side, step, pl.ds(group, 1), :]
                    block = unpack_block(mirrors[side][step, group], scale)
                    moved = pltpu.roll(block, ((column - spot_in + pack) % pack) * rows, 1)
                    total = jnp.where(lane == column, moved, total)
                tile = spot // tile_count
                other = spot - tile * tile_count
                target = pl.ds(pl.multiple_of(other * width, width), width)
                matrix[tile, :, target] = total

        return carry

    lax.fori_loop(0, table[base], transposed, 0)


def place_table(columns, kinds, sources, slots, share, chips, rows):
    blocks = share + extra_blocks(share, rows)
    behind = extra_blocks(share, rows) * rows
    spots = kinds.shape[0]
    wanted = jnp.concatenate([jnp.where(kinds == 1, sources, -1), slots])
    there = wanted >= 0
    chip = wanted // share
    inside = wanted % share
    block_at = jnp.where(there, chip * blocks + inside, 0)
    scale_at = jnp.where(there, chip * behind + inside, 2 * chips * behind)
    turned = kinds == 2
    spot_ids = jnp.arange(spots, dtype=jnp.int32)
    rank = jnp.sum((turned[None, :] & (spot_ids[None, :] < spot_ids[:, None])), axis=1)
    hot = turned[None, :] & (rank[None, :] == spot_ids[:, None])
    listed = jnp.sum(jnp.where(hot[None], jnp.stack([spot_ids, sources])[:, None], 0), axis=2)
    count = jnp.sum(turned.astype(jnp.int32)).reshape(1)
    table = jnp.concatenate([block_at, scale_at, count, listed.reshape(-1), columns])
    return table.astype(jnp.int32)


def place(table, directs, mirrors, share, here, tile_count, slot_count):
    chips, blocks, rows, width = directs[0].shape
    pack = mirrors[0].shape[0]
    groups = chips * share // pack
    behind = extra_blocks(share, rows) * rows
    direct = jnp.concatenate(directs, axis=0).reshape(2 * chips * blocks, rows, width)
    return pl.pallas_call(
        functools.partial(place_kernel, share, chips),
        out_shape=(
            jax.ShapeDtypeStruct((here, rows, tile_count * width), jnp.float32),
            jax.ShapeDtypeStruct((1, slot_count, rows, width), jnp.float32),
        ),
        grid_spec=pltpu.PrefetchScalarGridSpec(
            num_scalar_prefetch=1,
            grid=(),
            in_specs=[VMEM_SPEC] * 3,
            out_specs=[VMEM_SPEC] * 2,
            scratch_shapes=[
                pltpu.VMEM((2 * chips * behind + rows, width), jnp.float32),
                pltpu.VMEM((2, pack) + scale_scratch(groups, rows, width).shape, jnp.float32),
            ],
        ),
        cost_estimate=TINY,
        compiler_params=PARAMS,
    )(table, direct, *mirrors)


def take(value, index):
    return lax.dynamic_index_in_dim(value, index, 0, keepdims=False)


def body(factors, pairs, shared, owners):
    aux_rows, here, orbitals, width = factors.shape
    pair_size = lax.axis_size("pair")
    aux_size = lax.axis_size("aux")
    chips = pair_size // 2
    tile_count = here * pair_size
    pair_count = pairs.shape[0]
    rows = width // aux_size
    slot_count = 4 * (pair_count // pair_size)
    me = lax.axis_index("pair")
    core = me % 2
    chip = me // 2
    column = lax.axis_index("aux")
    depth = aux_rows // pair_size
    pack = aux_size
    unit = max(pack, chips)
    half = -(-(-(-pair_count // 2)) // unit) * unit
    share = half // chips
    padded = 2 * half

    pair_ids = jnp.arange(pair_count, dtype=jnp.int32)
    lefts, rights = pairs[:, 0], pairs[:, 1]
    same_owner = owners[:, None] == owners[None, :]
    rank = jnp.sum(
        (same_owner & (pair_ids[None, :] < pair_ids[:, None])).astype(jnp.int32), axis=1
    )
    tile_ids = jnp.arange(tile_count, dtype=jnp.int32)
    all_chips = jnp.arange(chips, dtype=jnp.int32)[:, None]
    steps_away = (tile_ids // (2 * here)) ^ all_chips
    is_last = (steps_away == chips - 1).astype(jnp.int32)
    group_of = is_last + is_last * (tile_ids % here == here - 1)
    left_hot = (lefts[:, None] == tile_ids).astype(jnp.int32)
    right_hot = (rights[:, None] == tile_ids).astype(jnp.int32)
    left_group = jnp.sum(left_hot[None] * group_of[:, None], axis=2)
    right_group = jnp.sum(right_hot[None] * group_of[:, None], axis=2)
    ready_at = jnp.maximum(left_group, right_group)
    arrival = ((tile_ids // here) ^ me) * here + tile_ids % here
    left_slots = jnp.sum(left_hot * arrival, axis=1)
    right_slots = jnp.sum(right_hot * arrival, axis=1)
    ready = take(ready_at, chip)

    real_half = -(-pair_count // 2)
    all_pairs = tile_count * (tile_count + 1) // 2
    bounds, enough = [0], jnp.bool_(True)
    stage_of = [here - 1]
    for stage in stage_of:
        known = tile_count - 2 * (here - stage)
        part = known * (known + 1) / 2 / all_pairs
        spread = (real_half * part * (1 - part) * (1 - real_half / all_pairs)) ** 0.5
        early = int(real_half * part - 3.75 * spread)
        bounds.append(early)
        ahead = (ready_at <= (stage if here > 1 else 0)).astype(jnp.int32)
        ahead = jnp.pad(ahead, ((0, 0), (0, padded - pair_count)))
        enough &= jnp.all(jnp.sum(ahead.reshape(chips, 2, half), axis=2) >= early)
    bounds.append(half)

    values = jnp.stack([left_slots, right_slots, shared[:, 0], ready])
    values = jnp.pad(values, ((0, 0), (0, padded - pair_count)))
    values = values.at[3, pair_count:].set(64) if padded > pair_count else values
    values = values.reshape(4, 2, half)
    local_ids = jnp.arange(half, dtype=jnp.int32)
    target_of = ((local_ids // share) ^ chip) * share + local_ids % share
    key = values[3] * half + local_ids
    spot_of = jnp.sum((key[:, None, :] < key[:, :, None]).astype(jnp.int32), axis=2)
    sorter = spot_of[:, None, :] == local_ids[:, None]
    fields = jnp.concatenate([values[:3], jnp.broadcast_to(target_of, (1, 2, half))])
    fields = jnp.sum(jnp.where(sorter[None], fields[:, :, None, :], 0), axis=3).astype(jnp.int32)
    mine = take(jnp.swapaxes(fields, 0, 1), core)
    theirs = take(jnp.swapaxes(fields, 0, 1), 1 - core)

    local = pair_ids % half
    part_core = pair_ids // half
    final_pos = (part_core ^ core) * half + ((local // share) ^ chip) * share + local % share
    my_rows = me * here + jnp.arange(here, dtype=jnp.int32)
    others = jnp.arange(tile_count, dtype=jnp.int32)
    is_direct = (lefts == my_rows[:, None, None]) & (rights == others[None, :, None])
    is_mirror = (rights == my_rows[:, None, None]) & (lefts == others[None, :, None])
    any_direct = jnp.any(is_direct, axis=-1)
    any_mirror = jnp.any(is_mirror, axis=-1)
    kinds = jnp.where(any_direct, 1, jnp.where(any_mirror, 2, 0)).astype(jnp.int32).reshape(-1)
    chosen = jnp.where(any_direct[..., None], is_direct, is_mirror)
    sources = jnp.sum(jnp.where(chosen, final_pos, 0), axis=-1).astype(jnp.int32).reshape(-1)
    slot_ids = jnp.arange(slot_count, dtype=jnp.int32)
    matches = (owners[None, :] == me) & (rank[None, :] == slot_ids[:, None])
    slots = jnp.sum(jnp.where(matches, final_pos + 1, 0), axis=1).astype(jnp.int32) - 1
    columns = column ^ jnp.arange(aux_size, dtype=jnp.int32)
    table = place_table(columns, kinds, sources, slots, share, chips, rows)

    def piece(step, low, high, *earlier):
        source = lax.optimization_barrier((factors, earlier))[0] if earlier else factors
        start = ((me ^ step) * depth, low, 0, 0)
        return lax.dynamic_slice(source, start, (depth, high - low, orbitals, width))

    last = [pair_size - 2, pair_size - 1]
    far = [(step, 0, here) for step in range(pair_size - 3, 3, -1)]
    far += [(step, inner, inner + 1) for inner in range(here) for step in last]
    sent, order = {}, []
    for spot, (step, low, high) in enumerate(far):
        gate = [order[0]] if spot >= 2 else [first] if spot else []
        block = piece(step, low, high, *gate)
        sent[step, low] = swap(block, "pair", pair_size, step)
        order.append(sent[step, low])
        if spot == 0:
            first = block
    for step in (3, 2, 1):
        sent[step, 0] = swap(piece(step, 0, here, first), "pair", pair_size, step)
    sent[0, 0] = piece(0, 0, here, first)
    parts = [
        [key for key in sent if key[0] not in last or key[1] < stage] for stage in stage_of
    ] + [list(sent)]

    def chip_blocks(keys, low, high, *earlier):
        given = [(step * here + inner, sent[step, inner]) for step, inner in keys]
        away = contract(given, theirs[:3, low:high], column, tile_count, aux_size, earlier)
        kept = contract(given, mine[:3, low:high], column, tile_count, aux_size, (away,))
        own, *others = split_columns(kept, swap(away, "pair", pair_size, 1))
        return [own] + [
            swap(other, "aux", aux_size, step + 1) for step, other in enumerate(others)
        ], kept

    groups, earlier = [], (table, mine, theirs, enough.astype(jnp.int32).reshape(1))
    for keys, low, high in zip(parts, bounds[:-1], bounds[1:]):
        group, kept = chip_blocks(keys, low, high, *earlier)
        groups.append(group)
        earlier = (group[0],)
    shares = lax.cond(
        enough,
        lambda: list(combine(mine[3], groups, share, True)),
        lambda: list(combine(mine[3], [chip_blocks(list(sent), 0, half)[0]], share, True)),
    )

    line = [shares[0]] + [
        swap(shares[step], "pair", pair_size, 2 * step) for step in range(1, chips)
    ]
    total = combine(None, [line], share, False)[0]
    line = [total] + [swap(total, "pair", pair_size, 2 * step) for step in range(1, chips)]
    own_direct = jnp.stack(line)
    other_direct = swap(own_direct, "pair", pair_size, 1)

    turned = turn(column, line, share)
    own_mirror = jnp.stack(
        [turned[0]] + [swap(turned[step], "aux", aux_size, step) for step in range(1, aux_size)]
    )
    other_mirror = swap(own_mirror, "pair", pair_size, 1)
    directs, mirrors = (own_direct, other_direct), (own_mirror, other_mirror)
    return place(table, directs, mirrors, share, here, tile_count, slot_count)


def solution(mesh):
    placed = (P("aux", "pair", None, None), P(), P(None, "aux"), P())
    return jax.shard_map(
        body,
        mesh=mesh,
        in_specs=placed,
        out_specs=(P("pair", "aux", None), P("pair", None, "aux", None)),
        check_vma=False,
    )
```
